128 devices in a mesh: pix: 64 (over x, z, y_hi, core), col: 2 (over y_lo).
Axes of the slice: x: 4, y: 4 (y_hi: 2, y_lo: 2; y = y_hi * 2 + y_lo), z: 4, core: 2. Of those that a mesh axis runs over, the one named last changes fastest.
Arguments:
- observed: float32 [16384, 4096], P('pix', 'col'), may hold values from -40 to 40
- valid_mask: int32 [16384, 512], P('pix', 'col'), may hold values 0 or 1
- pix_factor: float32 [16384, 256], P('pix'), may hold values from -6 to 6
- col_factor: float32 [4096, 256], P('col'), may hold values from -0.375 to 0.375
Outputs:
- pix_next: float32 [16384, 256], P('pix')
- col_next: float32 [4096, 256], P('col')
- cloud: float32 [16384, 4096], P('pix', 'col')
The draws below stay inside these ranges and needn't reach their ends.
All inputs are finite; a program needn't handle non-finite values. No bound on the sum of `valid_mask` on one device may be relied on, other than what follows from the above.
Results may differ from the reference program's by a relative error of at most 0.0003.
Values sent between devices are 32-bit elements; how exact they have to be, the bound alone decides.
A program may use at most 64 MiB of HBM per device.

```python
import jax
import jax.numpy as jnp
from jax import lax

C = 4096
R = 256
BANDS = 8
WIDTH = 256
ITERS = 2
PASSES = 2
P_SIZE = 16384
DATES = 512


def draw_observed(key, part):
    key_rows, key_cols, key_noise = jax.random.split(jax.random.fold_in(key, 11), 3)
    row_scale = jnp.exp(jax.random.uniform(key_rows, (P_SIZE, 1), jnp.float32, jnp.log(0.2), jnp.log(2.0)))
    ramp = 3.0 ** (jnp.arange(P_SIZE, dtype=jnp.float32) / (P_SIZE - 1))
    col_scale = jnp.exp(jax.random.uniform(key_cols, (1, C), jnp.float32, jnp.log(0.2), jnp.log(2.0)))
    noise = jnp.clip(jax.random.normal(key_noise, (P_SIZE, C), jnp.float32), -3.3, 3.3)
    values = 0.5 * row_scale * ramp[:, None] * col_scale * noise
    return jnp.clip(values, -40.0, 40.0).astype(jnp.float32)


def plant(entries, key, low, high):
    shape = entries.shape
    place = [jax.random.randint(jax.random.fold_in(key, axis), (), 0, shape[axis]) for axis in range(len(shape))]
    entries = entries.at[tuple(place)].set(low)
    longest = shape.index(max(shape))
    place[longest] = (place[longest] + 1) % shape[longest]
    return entries.at[tuple(place)].set(high)


def shard_levels(rng, shape, shards, least, largest):
    def one(dim, blocks):
        heights = jax.random.uniform(jax.random.fold_in(jax.random.fold_in(rng, 6), dim), (blocks,), jnp.float32, least / len(shards), largest / len(shards))
        return jnp.repeat(jnp.exp(heights), shape[dim] // blocks).reshape((-1,) + (1,) * (len(shape) - dim - 1))

    loudness = one(*shards[0])
    for cut in shards[1:]:
        loudness = loudness * one(*cut)
    return loudness


def scatter_about(key, shape, deviation, limit, pieces=(), kind=jnp.bfloat16):
    array = deviation * jax.random.normal(key, shape, jnp.float32)
    if pieces:
        array = array * shard_levels(key, shape, pieces, -0.22, 0.18)
    return jnp.clip(array, -limit, limit).astype(kind)


def setup_inputs(seed: int = 0) -> dict:
    arg_keys = jax.random.split(jax.random.key(seed), 5)
    observed = draw_observed(jax.random.fold_in(arg_keys[4], 71), 0)
    valid_mask = plant((jax.random.randint(arg_keys[1], (P_SIZE, DATES), 0, 10) < 7).astype(jnp.int32), jax.random.fold_in(arg_keys[1], 1), 0, 1)
    pix_factor = scatter_about(arg_keys[2], (P_SIZE, R), 1.0, 6.0, ((0, 64),), jnp.float32)
    col_factor = scatter_about(arg_keys[3], (C, R), R ** -0.5, 0.375, ((0, 2),), jnp.float32)
    return {"observed": observed, "valid_mask": valid_mask, "pix_factor": pix_factor, "col_factor": col_factor}


highest = lax.Precision.HIGHEST
threshold_scale = 1.0
diffusion = 0.2

def soft_cut(values, level):
    return jnp.sign(values) * jnp.maximum(jnp.abs(values) - level, 0.0)

def flux_of(diff, level):
    return diff / (1.0 + (diff / level) ** 2)

def level_of(residual, weight, total):
    return threshold_scale * jnp.sqrt(jnp.sum(weight * residual * residual) / total + 1e-06)

def reference(observed, valid_mask, pix_factor, col_factor):
    weight = jnp.repeat(valid_mask.astype(jnp.float32), BANDS, axis=1)
    total = float(observed.shape[0] * observed.shape[1])
    pix_fac = pix_factor
    col_fac = col_factor
    low_rank = jnp.dot(pix_fac, col_fac.T, precision=highest)
    for iteration in range(ITERS):
        residual = observed - low_rank
        level = level_of(residual, weight, total)
        sparse = weight * soft_cut(residual, level)
        misfit = weight * (sparse - residual)
        pix_grad = jnp.dot(misfit, col_fac, precision=highest)
        change = jnp.dot(pix_grad, col_fac.T, precision=highest)
        step_pix = jnp.sum(pix_grad * pix_grad) / jnp.sum(weight * change * change)
        pix_fac = pix_fac - step_pix * pix_grad
        low_rank = low_rank - step_pix * change
        misfit = weight * (sparse - (observed - low_rank))
        col_grad = jnp.dot(misfit.T, pix_fac, precision=highest)
        shifted = jnp.dot(pix_fac, col_grad.T, precision=highest)
        step_col = jnp.sum(col_grad * col_grad) / jnp.sum(weight * shifted * shifted)
        col_fac = col_fac - step_col * col_grad
        low_rank = low_rank - step_col * shifted
    residual = observed - low_rank
    level = level_of(residual, weight, total)
    layer = weight * soft_cut(residual, level)
    grid = layer.reshape(observed.shape[0] // WIDTH, WIDTH, -1)
    for sweep_index in range(PASSES):
        padded = jnp.pad(grid, ((1, 1), (1, 1), (0, 0)), mode='edge')
        summed = flux_of(padded[:-2, 1:-1] - grid, level) + flux_of(padded[2:, 1:-1] - grid, level)
        summed = summed + flux_of(padded[1:-1, :-2] - grid, level) + flux_of(padded[1:-1, 2:] - grid, level)
        grid = grid + diffusion * summed
    cloud = grid.reshape(layer.shape)
    return (pix_fac, col_fac, cloud)
```

```python
import functools

import jax
import jax.numpy as jnp
from jax import lax
from jax.experimental import pallas as pl
from jax.experimental.pallas import tpu as pltpu
from jax.sharding import PartitionSpec as P

BANDS = 8
WIDTH = 256
ITERS = 2
PASSES = 2
TILE = 256
TILES = 8
TOTAL = 67108864.0
diffusion = 0.2

f32 = jnp.float32
bf16 = jnp.bfloat16
MESH = pl.DeviceIdType.MESH


def split(x):
    hi = x.astype(bf16)
    return hi, (x - hi.astype(f32)).astype(bf16)


def mm(a, b):
    return lax.dot_general(a, b, (((1,), (0,)), ((), ())), preferred_element_type=f32)


def mm_nt(a, b):
    return lax.dot_general(a, b, (((1,), (1,)), ((), ())), preferred_element_type=f32)


def fold(x):
    part = x.reshape(x.shape[0] // 8, 8, x.shape[1]).sum(axis=0)
    return part[:, :128] + part[:, 128:]


def pack(*parts):
    rows = [jnp.sum(part, axis=0, keepdims=True) for part in parts]
    rows.append(jnp.zeros((8 - len(rows), 128), f32))
    return jnp.concatenate(rows, axis=0)


def factor_kernel(
    obs_in, mask_in, u_in, v_in,
    u_out, v_out, layer_out, level_out,
    r, w, c, vt, vs, hp, hsib, hf, vio, lay, mask, spread,
    u, us, uts, gp, gr, gs,
    f1p, f1m, n1p, n1m, f2p, f2m, n2p, n2m, ybuf,
    s1, s2, lev,
    in_sem, out_sem, ss1, rs1, ss2, rs2, gss, grs, sibs, sibr,
    r1s, r1r, r2s, r2r, ys, yr, a2s, a2r, a1s, a1r, fs, fr,
):
    p = lax.axis_index("pix")
    lo = lax.axis_index("col")
    core, h, z, x = p % 2, (p // 2) % 2, (p // 4) % 4, p // 16

    def dev(x, z, h, core, lo):
        return {"pix": ((x * 4 + z) * 2 + h) * 2 + core, "col": lo}

    i1 = (h * 2 + core) * 2 + lo
    i2 = x * 4 + z

    def peer1(d):
        j = (i1 + d) % 8
        return dev(x, z, j // 4, (j // 2) % 2, j % 2)

    def peer2(d):
        j = (i2 + d) % 16
        return dev(j // 4, j % 4, h, core, lo)

    sibling = dev(x, z, h, 1 - core, lo)
    col_pair = dev(x, z, h, core, 1 - lo)
    y_pair = dev(x, z, 1 - h, core, lo)
    q1 = x + core * (z - x)
    q2 = z + core * (x - z)

    def ring1(q):
        return dev(q + core * (x - q), z + core * (q - z), h, core, lo)

    def ring2(q):
        return dev(x + core * (q - x), q + core * (z - q), h, core, lo)

    def rcopy(src, dst, send, recv, to):
        return pltpu.make_async_remote_copy(
            src_ref=src, dst_ref=dst, send_sem=send, recv_sem=recv, device_id=to, device_id_type=MESH
        )

    barrier = pltpu.get_barrier_semaphore()
    for d in range(1, 8):
        pl.semaphore_signal(barrier, inc=1, device_id=peer1(d), device_id_type=MESH)
    for d in range(1, 16):
        pl.semaphore_signal(barrier, inc=1, device_id=peer2(d), device_id_type=MESH)

    def tile_cols(t):
        return pl.ds(pl.multiple_of(t * TILE, TILE), TILE)

    loads = [pltpu.make_async_copy(v_in.at[pl.ds(t * TILE, TILE)], vio.at[t], in_sem.at[t]) for t in range(TILES)]
    loads.append(pltpu.make_async_copy(u_in, u, in_sem.at[TILES]))
    loads.append(pltpu.make_async_copy(mask_in, mask, in_sem.at[TILES + 1]))
    for t in range(TILES):
        loads.append(
            pltpu.make_async_copy(obs_in.at[:, pl.ds(t * TILE, TILE)], r.at[t], in_sem.at[TILES + 2 + t])
        )
    for load in loads:
        load.start()
    for part in range(4):
        date = lax.broadcasted_iota(jnp.int32, (128, TILE), 0)
        column = lax.broadcasted_iota(jnp.int32, (128, TILE), 1) + part * TILE
        gap = column - date * BANDS
        spread[part] = jnp.where((gap >= 0) & (gap < BANDS), 1.0, 0.0).astype(bf16)
    for load in loads[: TILES]:
        load.wait()

    def turn_v(t, _):
        vt_t = jnp.transpose(vio[t])
        vt[t] = vt_t
        hi, low = split(vt_t)
        vs[t, 0] = hi
        vs[t, 1] = low
        return 0

    lax.fori_loop(0, TILES, turn_v, 0)
    for load in loads[TILES:]:
        load.wait()

    def set_u(value):
        u[...] = value
        hi, low = split(value)
        us[0] = hi
        us[1] = low

    set_u(u[...])

    def dot3(a_ref, hi, low):
        return mm(a_ref[0], hi) + mm(a_ref[0], low) + mm(a_ref[1], hi)

    def first(t, acc):
        dates = mask[:, pl.ds(pl.multiple_of((t // 4) * 128, 128), 128)].astype(f32).astype(bf16)
        w_t = mm(dates, spread[t % 4])
        w[t] = w_t
        r_t = w_t * (r[t] - dot3(us, vs[t, 0], vs[t, 1]))
        r[t] = r_t
        return acc + fold(r_t * r_t)

    zero = jnp.zeros((8, 128), f32)
    square = lax.fori_loop(0, TILES, first, zero)
    pl.semaphore_wait(barrier, 22)

    def all_reduce(k, message):
        s1[k, i1] = message
        for d in range(1, 8):
            rcopy(s1.at[k, i1], s1.at[k, i1], ss1.at[k], rs1.at[k], peer1(d)).start()
        whole = s1.at[k, pl.ds(0, 7)]
        done = rcopy(whole, whole, ss1.at[k], rs1.at[k], sibling)
        done.wait_recv()
        total = s1[k, 0]
        for j in range(1, 8):
            total = total + s1[k, j]
        s2[k, i2] = total
        for d in range(1, 16):
            rcopy(s2.at[k, i2], s2.at[k, i2], ss2.at[k], rs2.at[k], peer2(d)).start()
        done.wait_send()
        whole = s2.at[k, pl.ds(0, 15)]
        done = rcopy(whole, whole, ss2.at[k], rs2.at[k], ring1((q1 + 1) % 4))
        done.wait_recv()
        total = s2[k, 0]
        for j in range(1, 16):
            total = total + s2[k, j]
        done.wait_send()
        return jnp.sum(total, axis=1, keepdims=True)

    def level_from(square):
        return jnp.sqrt(jnp.maximum(square, 0.0) / TOTAL + 1e-06)

    sums = all_reduce(0, pack(square))
    lev[...] = jnp.broadcast_to(level_from(sums[0:1]), (8, 128))

    def cut(value, level):
        return jnp.minimum(jnp.maximum(value, -level), level)

    def ring_reduce(blk, rows, q, ring, fp, fm, np_, nm, sends, recvs):
        half = rows // 2
        plus, minus = ring((q + 1) % 4), ring((q + 3) % 4)
        kp, km, kf = (q + 1) % 4, (q + 3) % 4, (q + 2) % 4
        c1 = rcopy(blk(kf, 0, half), fp, sends.at[0], recvs.at[0], plus)
        c2 = rcopy(blk(kf, half, half), fm, sends.at[1], recvs.at[1], minus)
        c3 = rcopy(blk(kp, half, half), np_.at[pl.ds(half, half)], sends.at[2], recvs.at[2], plus)
        c4 = rcopy(blk(km, 0, half), nm.at[pl.ds(0, half)], sends.at[3], recvs.at[3], minus)
        for copy in (c1, c2, c3, c4):
            copy.start()
        c1.wait_recv()
        ref = blk(kp, 0, half)
        ref[...] = ref[...] + fp[...]
        c5 = rcopy(ref, np_.at[pl.ds(0, half)], sends.at[4], recvs.at[4], plus)
        c5.start()
        c2.wait_recv()
        ref = blk(km, half, half)
        ref[...] = ref[...] + fm[...]
        c6 = rcopy(ref, nm.at[pl.ds(half, half)], sends.at[5], recvs.at[5], minus)
        c6.start()
        for copy in (c3, c4, c5, c6):
            copy.wait_recv()
        ref = blk(q, 0, rows)
        ref[...] = ref[...] + np_[...] + nm[...]
        for copy in (c1, c2, c3, c4, c5, c6):
            copy.wait_send()

    def ring_gather(blk, rows, q, ring, sends, recvs, on_block):
        half = rows // 2
        plus, minus = ring((q + 1) % 4), ring((q + 3) % 4)
        kp, km, kf = (q + 1) % 4, (q + 3) % 4, (q + 2) % 4
        own = blk(q, 0, rows)
        c1 = rcopy(own, own, sends.at[0], recvs.at[0], plus)
        c2 = rcopy(own, own, sends.at[1], recvs.at[1], minus)
        c1.start()
        c2.start()
        on_block(0, blk(q, 0, rows))
        rcopy(own, blk(km, 0, rows), sends.at[0], recvs.at[0], plus).wait_recv()
        ref = blk(km, 0, half)
        c3 = rcopy(ref, ref, sends.at[2], recvs.at[2], plus)
        c3.start()
        on_block(1, blk(km, 0, rows))
        rcopy(own, blk(kp, 0, rows), sends.at[1], recvs.at[1], plus).wait_recv()
        ref = blk(kp, half, half)
        c4 = rcopy(ref, ref, sends.at[3], recvs.at[3], minus)
        c4.start()
        on_block(2, blk(kp, 0, rows))
        rcopy(ref, blk(kf, 0, half), sends.at[2], recvs.at[2], plus).wait_recv()
        rcopy(ref, blk(kf, half, half), sends.at[3], recvs.at[3], minus).wait_recv()
        on_block(3, blk(kf, 0, rows))
        for copy in (c1, c2, c3, c4):
            copy.wait_send()

    def iteration(it, _):
        level = lev[0:1, 0:1]

        copies = []
        for part in range(2):
            rows = pl.ds(part * 128, 128)

            def grow(t, acc):
                hi, low = split(cut(r[t, rows, :], level))
                v_hi, v_low = vs[t, 0], vs[t, 1]
                return acc + mm_nt(hi, v_hi) + mm_nt(hi, v_low) + mm_nt(low, v_hi)

            gp[rows, :] = lax.fori_loop(0, TILES, grow, jnp.zeros((128, TILE), f32))
            copies.append(rcopy(gp.at[rows], gr.at[rows], gss.at[part], grs.at[part], col_pair))
            copies[-1].start()
        for copy in copies:
            copy.wait()
        g = gp[...] + gr[...]
        gp[...] = g
        hi, low = split(g)
        gs[0] = hi
        gs[1] = low

        def curve(t, acc):
            c_t = w[t] * dot3(gs, vs[t, 0], vs[t, 1])
            c[t] = c_t
            return acc + fold(c_t * c_t)

        bottom = lax.fori_loop(0, TILES, curve, zero)
        sums = all_reduce(1 + 2 * it, pack(fold(g * g) * 0.5, bottom))
        step = sums[0:1] / sums[1:2]
        set_u(u[...] + step * gp[...])
        hi, low = split(jnp.transpose(u[...]))
        uts[0] = hi
        uts[1] = low

        def pull(t):
            r_t, ac = r[t], step * c[t]
            r[t] = r_t - ac
            hi, low = split(cut(r_t, level) - ac)
            hp[t] = dot3(uts, hi, low)

        first_tile = 4 * (1 - core)

        def pull_other(i, _):
            k = (q2 + 2 + i) % 4
            pull(first_tile + k)
            rcopy(hp.at[first_tile + k], hsib.at[k], sibs.at[k], sibr.at[k], sibling).start()
            return 0

        lax.fori_loop(0, 4, pull_other, 0)
        mine = 4 * core

        def pull_own(i, _):
            pull(mine + (q1 + 2 + i) % 4)
            return 0

        lax.fori_loop(0, 4, pull_own, 0)

        def join(i, _):
            k = (q1 + 2 + i) % 4
            rcopy(hp.at[first_tile + k], hsib.at[k], sibs.at[k], sibr.at[k], sibling).wait_recv()
            hp[mine + k] = hp[mine + k] + hsib[k]
            return 0

        lax.fori_loop(0, 4, join, 0)

        def blk1(k, start, rows):
            return hp.at[mine + k, pl.ds(start, rows)]

        ring_reduce(blk1, 256, q1, ring1, f1p, f1m, n1p, n1m, r1s, r1r)

        def blk2(k, start, rows):
            return hp.at[mine + q1, pl.ds(pl.multiple_of(64 * k + start, 32), rows)]

        ring_reduce(blk2, 64, q2, ring2, f2p, f2m, n2p, n2m, r2s, r2r)
        own = blk2(q2, 0, 64)
        copy = rcopy(own, ybuf, ys, yr, y_pair)
        copy.start()
        copy.wait()
        piece = own[...] + ybuf[...]
        hf[mine + q1, pl.ds(pl.multiple_of(64 * q2, 64), 64), :] = piece
        norm = fold(piece * piece) * 0.5

        def fblk2(k, start, rows):
            return hf.at[mine + q1, pl.ds(pl.multiple_of(64 * k + start, 32), rows)]

        ring_gather(fblk2, 64, q2, ring2, a2s, a2r, lambda i, ref: None)

        def fblk1(k, start, rows):
            return hf.at[mine + k, pl.ds(start, rows)]

        def hand_over(i, ref):
            rcopy(ref, ref, fs.at[i], fr.at[i], sibling).start()

        ring_gather(fblk1, 256, q1, ring1, a1s, a1r, hand_over)

        def shift(t, accs):
            hi, low = split(hf[t])
            s_t = w[t] * dot3(us, hi, low)
            c[t] = s_t
            r_t = r[t]
            a0, a1, a2 = accs
            return a0 + fold(r_t * r_t), a1 + fold(r_t * s_t), a2 + fold(s_t * s_t)

        accs = lax.fori_loop(0, 4, lambda i, accs: shift(mine + i, accs), (zero, zero, zero))
        for i in range(4):
            ref = hf.at[first_tile + i]
            wait = rcopy(ref, ref, fs.at[i], fr.at[i], sibling)
            wait.wait_recv()
        for i in range(4):
            ref = hf.at[first_tile + i]
            rcopy(ref, ref, fs.at[i], fr.at[i], sibling).wait_send()
            rcopy(hp.at[first_tile + i], hsib.at[i], sibs.at[i], sibr.at[i], sibling).wait_send()
        accs = lax.fori_loop(0, 4, lambda i, accs: shift(first_tile + i, accs), accs)
        sums = all_reduce(2 + 2 * it, pack(norm, *accs))
        step = sums[0:1] / sums[3:4]
        square = sums[1:2] - 2.0 * step * sums[2:3] + step * step * sums[3:4]
        lev[...] = jnp.broadcast_to(level_from(square), (8, 128))

        def update(t, _):
            v_t = vt[t] + step * hf[t]
            vt[t] = v_t
            hi, low = split(v_t)
            vs[t, 0] = hi
            vs[t, 1] = low
            r[t] = r[t] - step * c[t]
            return 0

        lax.fori_loop(0, TILES, update, 0)
        return 0

    lax.fori_loop(0, ITERS, iteration, 0)
    level = lev[0:1, 0:1]

    def finish(t, _):
        r_t = r[t]
        lay[t] = r_t - cut(r_t, level)
        vio[t] = jnp.transpose(vt[t])
        return 0

    lax.fori_loop(0, TILES, finish, 0)
    stores = [pltpu.make_async_copy(u, u_out, out_sem.at[0]), pltpu.make_async_copy(lev, level_out, out_sem.at[1])]
    for t in range(TILES):
        stores.append(pltpu.make_async_copy(vio.at[t], v_out.at[pl.ds(t * TILE, TILE)], out_sem.at[2 + t]))
        stores.append(
            pltpu.make_async_copy(lay.at[t], layer_out.at[:, pl.ds(t * TILE, TILE)], out_sem.at[2 + TILES + t])
        )
    for store in stores:
        store.start()
    for store in stores:
        store.wait()


def factors(observed, valid_mask, pix_factor, col_factor):
    any_space = pl.BlockSpec(memory_space=pl.ANY)
    full = pltpu.VMEM((TILES, TILE, TILE), f32)
    square = pltpu.VMEM((TILE, TILE), f32)
    dma = pltpu.SemaphoreType.DMA
    return pl.pallas_call(
        factor_kernel,
        out_shape=(
            jax.ShapeDtypeStruct((256, 256), f32),
            jax.ShapeDtypeStruct((2048, 256), f32),
            jax.ShapeDtypeStruct((256, 2048), f32),
            jax.ShapeDtypeStruct((8, 128), f32),
        ),
        in_specs=[any_space] * 4,
        out_specs=[any_space] * 4,
        scratch_shapes=[
            full, full, full, full,
            pltpu.VMEM((TILES, 2, TILE, TILE), bf16),
            full,
            pltpu.VMEM((4, TILE, TILE), f32),
            full, full, full,
            pltpu.VMEM((256, 256), jnp.int32),
            pltpu.VMEM((4, 128, TILE), bf16),
            square,
            pltpu.VMEM((2, TILE, TILE), bf16),
            pltpu.VMEM((2, TILE, TILE), bf16),
            square, square,
            pltpu.VMEM((2, TILE, TILE), bf16),
            pltpu.VMEM((128, TILE), f32), pltpu.VMEM((128, TILE), f32), square, square,
            pltpu.VMEM((32, TILE), f32), pltpu.VMEM((32, TILE), f32),
            pltpu.VMEM((64, TILE), f32), pltpu.VMEM((64, TILE), f32),
            pltpu.VMEM((64, TILE), f32),
            pltpu.VMEM((5, 8, 8, 128), f32),
            pltpu.VMEM((5, 16, 8, 128), f32),
            pltpu.VMEM((8, 128), f32),
            dma((2 * TILES + 2,)), dma((2 * TILES + 2,)),
            dma((5,)), dma((5,)), dma((5,)), dma((5,)),
            dma((2,)), dma((2,)), dma((4,)), dma((4,)),
            dma((6,)), dma((6,)), dma((6,)), dma((6,)), dma, dma,
            dma((4,)), dma((4,)), dma((4,)), dma((4,)), dma((4,)), dma((4,)),
        ],
        compiler_params=pltpu.CompilerParams(
            collective_id=0, has_side_effects=True, vmem_limit_bytes=56 * 1024 * 1024
        ),
        name="factors",
    )(observed, valid_mask, pix_factor, col_factor)


def passed_along(block, axis, distance):
    devices = range(lax.axis_size(axis))
    route = [(i - distance, i) for i in devices if i - distance in devices]
    return lax.ppermute(block, axis, route)


def flux_of(diff, level):
    return diff / (1.0 + (diff / level) ** 2)


def smooth_pass(grid, level, strip_index, pix_count):
    has_north = strip_index > 0
    has_south = strip_index < pix_count - 1
    top_row = grid[0]
    bottom_row = grid[-1]
    north_rim = passed_along(bottom_row, "pix", 1)
    south_rim = passed_along(top_row, "pix", -1)
    north_rim = jnp.where(has_north, north_rim, top_row)
    south_rim = jnp.where(has_south, south_rim, bottom_row)
    north = jnp.concatenate([north_rim[None], grid[:-1]], axis=0)
    south = jnp.concatenate([grid[1:], south_rim[None]], axis=0)
    west = jnp.concatenate([grid[:, :1], grid[:, :-1]], axis=1)
    east = jnp.concatenate([grid[:, 1:], grid[:, -1:]], axis=1)
    summed = flux_of(north - grid, level) + flux_of(south - grid, level)
    summed = summed + flux_of(west - grid, level) + flux_of(east - grid, level)
    return grid + diffusion * summed


def per_device(observed, valid_mask, pix_factor, col_factor):
    pix_fac, col_fac, layer, level = factors(observed, valid_mask, pix_factor, col_factor)
    level = level[0, 0]
    pixels, columns = observed.shape
    strip_index = lax.axis_index("pix")
    grid = layer.reshape(pixels // WIDTH, WIDTH, columns)
    for sweep_index in range(PASSES):
        grid = smooth_pass(grid, level, strip_index, lax.axis_size("pix"))
    return (pix_fac, col_fac, grid.reshape(pixels, columns))


def solution(mesh):
    in_specs = (P("pix", "col"), P("pix", "col"), P("pix", None), P("col", None))
    out_specs = (P("pix", None), P("col", None), P("pix", "col"))
    return jax.shard_map(
        per_device, mesh=mesh, in_specs=in_specs, out_specs=out_specs, check_vma=False
    )
```

```python
import jax
import jax.numpy as jnp
from jax import lax
from jax.experimental import pallas as pl
from jax.experimental.pallas import tpu as pltpu
from jax.sharding import PartitionSpec as P

BANDS = 8
WIDTH = 256
ITERS = 2
TILE = 256
TILES = 8
CHUNKS = 16
TOTAL = 67108864.0
diffusion = 0.2

f32 = jnp.float32
bf16 = jnp.bfloat16
MESH = pl.DeviceIdType.MESH


def split(x):
    hi = x.astype(bf16)
    return hi, (x - hi.astype(f32)).astype(bf16)


def mm(a, b):
    return lax.dot_general(a, b, (((1,), (0,)), ((), ())), preferred_element_type=f32)


def mm_nt(a, b):
    return lax.dot_general(a, b, (((1,), (1,)), ((), ())), preferred_element_type=f32)


def fold(x):
    part = x.reshape(x.shape[0] // 8, 8, x.shape[1]).sum(axis=0)
    return part[:, :128] + part[:, 128:]


def pack(*parts):
    rows = [jnp.sum(part, axis=0, keepdims=True) for part in parts]
    rows.append(jnp.zeros((8 - len(rows), 128), f32))
    return jnp.concatenate(rows, axis=0)


def kernel(
    obs_in, mask_in, u_in, v_in,
    u_out, v_out, cloud_out,
    r, w, c, vt, vs, hp, hsib, hf, vio, lay, mask, spread,
    u, us, uts, gp, gr, gs, n1, n2, s1, s2, lev,
    hx, mh, uh, uhs, ya, yb, fb,
    in_sem, out_sem, ss1, rs1, ss2, rs2, gss, grs, sibs, sibr,
    r1s, r1r, r2s, r2r, a2s, a2r, a1s, a1r, fs, fr,
    hys, hyr, hzs, hzr, h1s, h1r, h2s, h2r,
):
    p = lax.axis_index("pix")
    lo = lax.axis_index("col")
    core, h, z, x = p % 2, (p // 2) % 2, (p // 4) % 4, p // 16

    def dev(x, z, h, core, lo):
        return {"pix": ((x * 4 + z) * 2 + h) * 2 + core, "col": lo}

    i1 = (h * 2 + core) * 2 + lo
    i2 = x * 4 + z

    def peer1(d):
        j = (i1 + d) % 8
        return dev(x, z, j // 4, (j // 2) % 2, j % 2)

    def peer2(d):
        j = (i2 + d) % 16
        return dev(j // 4, j % 4, h, core, lo)

    sibling = dev(x, z, h, 1 - core, lo)
    col_pair = dev(x, z, h, core, 1 - lo)
    y_pair = dev(x, z, 1 - h, core, lo)
    z_next = peer2(17 - 2 * h)
    q1 = x + core * (z - x)
    q2 = z + core * (x - z)
    iy = 2 + (h + core) % 2
    iz = 5 - iy

    def ring1(q):
        return dev(q + core * (x - q), z + core * (q - z), h, core, lo)

    def ring2(q, h):
        return dev(x + core * (q - x), q + core * (z - q), h, core, lo)

    def rcopy(src, dst, send, recv, to):
        return pltpu.make_async_remote_copy(
            src_ref=src, dst_ref=dst, send_sem=send, recv_sem=recv, device_id=to, device_id_type=MESH
        )

    def each(low, high, step):
        def body(i, _):
            step(i)
            return 0

        lax.fori_loop(low, high, body, 0)

    barrier = pltpu.get_barrier_semaphore()
    for d in range(1, 8):
        pl.semaphore_signal(barrier, inc=1, device_id=peer1(d), device_id_type=MESH)
    for d in range(1, 16):
        pl.semaphore_signal(barrier, inc=1, device_id=peer2(d), device_id_type=MESH)

    loads = [pltpu.make_async_copy(v_in.at[pl.ds(t * TILE, TILE)], vio.at[t], in_sem.at[t]) for t in range(TILES)]
    loads.append(pltpu.make_async_copy(u_in, u, in_sem.at[TILES]))
    loads.append(pltpu.make_async_copy(mask_in, mask, in_sem.at[TILES + 1]))
    for t in range(TILES):
        loads.append(
            pltpu.make_async_copy(obs_in.at[:, pl.ds(t * TILE, TILE)], r.at[t], in_sem.at[TILES + 2 + t])
        )
    for load in loads:
        load.start()
    for part in range(4):
        date = lax.broadcasted_iota(jnp.int32, (128, TILE), 0)
        column = lax.broadcasted_iota(jnp.int32, (128, TILE), 1) + part * TILE
        gap = column - date * BANDS
        spread[part] = jnp.where((gap >= 0) & (gap < BANDS), 1.0, 0.0).astype(bf16)

    MASK, PIX = CHUNKS, CHUNKS + 1

    def chunk(i):
        return i // 2, pl.ds(pl.multiple_of((i % 2) * 128, 128), 128)

    def y_obs(i, slot):
        t, rows = chunk(i)
        cols = pl.ds(pl.multiple_of(t * TILE, TILE), TILE)
        return rcopy(obs_in.at[rows, cols], hx.at[slot, t, rows], hys.at[i], hyr.at[i], y_pair)

    def z_obs(i):
        t, rows = chunk(i)
        return rcopy(hx.at[iy, t, rows], hx.at[iz, t, rows], hzs.at[i], hzr.at[i], z_next)

    def y_send(i):
        y_obs(i, iz).start()

    def z_send(i):
        y_obs(i, iy).wait_recv()
        z_obs(i).start()

    def y_mask(slot):
        return rcopy(mask_in, mh.at[slot], hys.at[MASK], hyr.at[MASK], y_pair)

    def y_pix(slot):
        return rcopy(u, uh.at[slot], hys.at[PIX], hyr.at[PIX], y_pair)

    z_mask = rcopy(mh.at[iy], mh.at[iz], hzs.at[MASK], hzr.at[MASK], z_next)
    z_pix = rcopy(uh.at[iy], uh.at[iz], hzs.at[PIX], hzr.at[PIX], z_next)
    s1_mask = rcopy(mask_in, mh.at[0], h1s.at[TILES], h1r.at[TILES], sibling)
    s1_pix = rcopy(u, uh.at[0], h1s.at[TILES + 1], h1r.at[TILES + 1], sibling)

    def s1_obs(t):
        cols = pl.ds(pl.multiple_of(t * TILE, TILE), TILE)
        return rcopy(obs_in.at[:, cols], hx.at[0, t], h1s.at[t], h1r.at[t], sibling)

    def s2_obs(t):
        return rcopy(hx.at[2, t], hx.at[1, t], h2s.at[t], h2r.at[t], sibling)

    s2_mask = rcopy(mh.at[2], mh.at[1], h2s.at[TILES], h2r.at[TILES], sibling)
    s2_pix = rcopy(uh.at[2], uh.at[1], h2s.at[TILES + 1], h2r.at[TILES + 1], sibling)

    pl.semaphore_wait(barrier, 22)
    y_mask(iz).start()
    y_send(0)
    s1_mask.start()
    each(0, TILES, lambda t: s1_obs(t).start())

    for load in loads[: TILES]:
        load.wait()

    def turn_v(t):
        vt_t = jnp.transpose(vio[t])
        vt[t] = vt_t
        hi, low = split(vt_t)
        vs[t, 0] = hi
        vs[t, 1] = low

    each(0, TILES, turn_v)
    for load in loads[TILES:]:
        load.wait()

    def set_u(value):
        u[...] = value
        hi, low = split(value)
        us[0] = hi
        us[1] = low

    set_u(u[...])

    def dot3(a_ref, hi, low):
        return mm(a_ref[0], hi) + mm(a_ref[0], low) + mm(a_ref[1], hi)

    def weight(mask_ref, t):
        dates = mask_ref[:, pl.ds(pl.multiple_of((t // 4) * 128, 128), 128)].astype(f32).astype(bf16)
        return mm(dates, spread[t % 4])

    def first(t, acc):
        w_t = weight(mask, t)
        w[t] = w_t
        r_t = w_t * (r[t] - dot3(us, vs[t, 0], vs[t, 1]))
        r[t] = r_t
        return acc + fold(r_t * r_t)

    zero = jnp.zeros((8, 128), f32)
    square = lax.fori_loop(0, TILES, first, zero)

    def all_reduce(k, message, between):
        s1[k, i1] = message
        for d in range(1, 8):
            rcopy(s1.at[k, i1], s1.at[k, i1], ss1.at[k], rs1.at[k], peer1(d)).start()
        whole = s1.at[k, pl.ds(0, 7)]
        done1 = rcopy(whole, whole, ss1.at[k], rs1.at[k], sibling)
        done1.wait_recv()
        total = s1[k, 0]
        for j in range(1, 8):
            total = total + s1[k, j]
        s2[k, i2] = total
        for d in range(1, 16):
            rcopy(s2.at[k, i2], s2.at[k, i2], ss2.at[k], rs2.at[k], peer2(d)).start()
        between()
        whole = s2.at[k, pl.ds(0, 15)]
        done2 = rcopy(whole, whole, ss2.at[k], rs2.at[k], ring1((q1 + 1) % 4))
        done2.wait_recv()
        total = s2[k, 0]
        for j in range(1, 16):
            total = total + s2[k, j]
        done1.wait_send()
        done2.wait_send()
        return jnp.sum(total, axis=1, keepdims=True)

    def level_from(square):
        return jnp.sqrt(jnp.maximum(square, 0.0) / TOTAL + 1e-06)

    sums = all_reduce(0, pack(square), lambda: each(1, 3, y_send))
    lev[...] = jnp.broadcast_to(level_from(sums[0:1]), (8, 128))
    y_mask(iy).wait_recv()
    z_mask.start()

    def cut(value, level):
        return jnp.minimum(jnp.maximum(value, -level), level)

    mine, other = 4 * core, 4 * (1 - core)

    def y_more(low, high):
        each(jnp.minimum(low, CHUNKS), jnp.minimum(high, CHUNKS), y_send)

    def iteration(it, _):
        level = lev[0:1, 0:1]
        y0, z0 = 3 + 10 * it, 4 * it

        each(z0, z0 + 2 * it, z_send)
        copies = []
        for part in range(2):
            rows = pl.ds(part * 128, 128)

            def grow(t, acc):
                hi, low = split(cut(r[t, rows, :], level))
                v_hi, v_low = vs[t, 0], vs[t, 1]
                return acc + mm_nt(hi, v_hi) + mm_nt(hi, v_low) + mm_nt(low, v_hi)

            gp[rows, :] = lax.fori_loop(0, TILES, grow, jnp.zeros((128, TILE), f32))
            copies.append(rcopy(gp.at[rows], gr.at[rows], gss.at[part], grs.at[part], col_pair))
            copies[-1].start()
        z1 = z0 + 2 * it
        each(z1, z1 + 2 + it, z_send)
        z2 = z1 + 2 + it
        for copy in copies:
            copy.wait()
        g = gp[...] + gr[...]
        gp[...] = g
        hi, low = split(g)
        gs[0] = hi
        gs[1] = low

        def curve(t, acc):
            c_t = w[t] * dot3(gs, vs[t, 0], vs[t, 1])
            c[t] = c_t
            return acc + fold(c_t * c_t)

        bottom = lax.fori_loop(0, TILES, curve, zero)
        z_send(z2)
        sums = all_reduce(1 + 2 * it, pack(fold(g * g) * 0.5, bottom), lambda: y_more(y0, y0 + 1))
        step = sums[0:1] / sums[1:2]
        set_u(u[...] + step * gp[...])
        hi, low = split(jnp.transpose(u[...]))
        uts[0] = hi
        uts[1] = low

        @pl.when(it == ITERS - 1)
        def _():
            y_pix(iz).start()
            s1_pix.start()

        y_more(y0 + 1, y0 + 5)

        def pull(t):
            r_t, ac = r[t], step * c[t]
            r[t] = r_t - ac
            hi, low = split(cut(r_t, level) - ac)
            hp[t] = dot3(uts, hi, low)

        def order(i):
            return jnp.where(i == 0, 2, jnp.where(i == 1, 1, jnp.where(i == 2, 3, 0)))

        def hand(k, slot):
            return rcopy(hp.at[other + k], hsib.at[slot], sibs.at[slot], sibr.at[slot], sibling)

        def reduce1(d):
            return rcopy(hp.at[mine + (q1 + d) % 4], n1.at[d - 1], r1s.at[d - 1], r1r.at[d - 1], ring1((q1 + d) % 4))

        def pull_step(i):
            @pl.when(i < 4)
            def _():
                d = order(i)
                pull(other + (q2 + d) % 4)
                hand((q2 + d) % 4, d).start()
                pull(mine + (q1 + d) % 4)

            @pl.when(i >= 2)
            def _():
                d = order(i - 2)
                hand(0, d).wait_recv()
                tile = mine + (q1 + d) % 4
                hp[tile] = hp[tile] + hsib[d]

                @pl.when(i < 5)
                def _():
                    reduce1(d).start()

        each(0, 6, pull_step)
        for d in (1, 3, 2):
            reduce1(d).wait_recv()
        tile = mine + q1
        hp[tile] = hp[tile] + n1[0] + n1[1] + n1[2]

        j2 = q2 * 2 + h

        def sub(ref, j):
            return ref.at[tile, pl.ds(pl.multiple_of(32 * j, 32), 32)]

        def reduce2(e):
            j = (j2 + e) % 8
            return rcopy(sub(hp, j), n2.at[e - 1], r2s.at[e - 1], r2r.at[e - 1], ring2(j // 2, j % 2))

        for e in range(1, 8):
            reduce2(e).start()

        @pl.when(it == ITERS - 1)
        def _():
            y_pix(iy).wait_recv()
            z_pix.start()

        for e in range(1, 8):
            reduce2(e).wait_recv()
        piece = sub(hp, j2)[...]
        for e in range(7):
            piece = piece + n2[e]
        sub(hf, j2)[...] = piece
        norm = fold(piece * piece)

        def gather2(e, j):
            to = (j2 + e) % 8
            return rcopy(sub(hf, j), sub(hf, j), a2s.at[e - 1], a2r.at[e - 1], ring2(to // 2, to % 2))

        for e in range(1, 8):
            gather2(e, j2).start()
        for e in range(1, 8):
            gather2(e, (j2 + 8 - e) % 8).wait_recv()

        def gather1(d, k):
            return rcopy(hf.at[mine + k], hf.at[mine + k], a1s.at[d - 1], a1r.at[d - 1], ring1((q1 + d) % 4))

        for d in (2, 1, 3):
            gather1(d, q1).start()
        y_more(y0 + 5, y0 + 9)

        def shift(t, accs):
            hi, low = split(hf[t])
            s_t = w[t] * dot3(us, hi, low)
            c[t] = s_t
            r_t = r[t]
            a0, a1, a2 = accs
            return a0 + fold(r_t * r_t), a1 + fold(r_t * s_t), a2 + fold(s_t * s_t)

        def pass_on(k, i, half):
            return rcopy(hf.at[half + k], hf.at[half + k], fs.at[i], fr.at[i], sibling)

        def shift_step(i, accs):
            d = jnp.where(i == 2, 3, jnp.where(i == 3, 2, i))
            k = (q1 + 4 - d) % 4

            @pl.when(i > 0)
            def _():
                gather1(d, k).wait_recv()

            pass_on(k, i, mine).start()
            accs = shift(mine + k, accs)
            k = (q2 + 4 - d) % 4
            pass_on(k, i, other).wait_recv()
            return shift(other + k, accs)

        accs = lax.fori_loop(0, 4, shift_step, (zero, zero, zero))
        for d in (1, 2, 3):
            reduce1(d).wait_send()
            gather1(d, q1).wait_send()
        for e in range(1, 8):
            reduce2(e).wait_send()
            gather2(e, j2).wait_send()
        for i in range(4):
            hand(i, i).wait_send()
            pass_on(i, i, mine).wait_send()
        z_send(z2 + 1)
        sums = all_reduce(2 + 2 * it, pack(norm, *accs), lambda: y_more(y0 + 9, y0 + 10))
        step = sums[0:1] / sums[3:4]
        square = sums[1:2] - 2.0 * step * sums[2:3] + step * step * sums[3:4]
        lev[...] = jnp.broadcast_to(level_from(square), (8, 128))

        @pl.when(it == ITERS - 1)
        def _():
            each(z2 + 2, CHUNKS, z_send)

        def update(t):
            v_t = vt[t] + step * hf[t]
            vt[t] = v_t
            hi, low = split(v_t)
            vs[t, 0] = hi
            vs[t, 1] = low
            r[t] = r[t] - step * c[t]

        each(0, TILES, update)
        return 0

    lax.fori_loop(0, ITERS, iteration, 0)
    stores = [pltpu.make_async_copy(u, u_out, out_sem.at[0])]
    stores[0].start()

    z_mask.wait_recv()
    s2_mask.start()
    z_pix.wait_recv()
    s2_pix.start()
    s1_mask.wait_recv()
    s1_pix.wait_recv()
    s2_mask.wait_recv()
    s2_pix.wait_recv()
    for k in range(4):
        hi, low = split(uh[k])
        uhs[k, 0] = hi
        uhs[k, 1] = low
    level = lev[0:1, 0:1]
    inverse = 1.0 / level
    last = 63
    side = 1 - 2 * core

    def flag(offset):
        row = p + offset
        return ((row >= 0) & (row <= last)).astype(f32)

    has1, has2, has3 = flag(-side), flag(2 * side), flag(-2 * side)

    def soft(scaled):
        return scaled - jnp.minimum(jnp.maximum(scaled, -1.0), 1.0)

    def g(e):
        return e / (1.0 + e * e)

    def ready(t):
        z_obs(2 * t).wait_recv()
        z_obs(2 * t + 1).wait_recv()
        s2_obs(t).start()

    STRIP = 32
    AT = 8

    def rim(ref):
        ref[AT - 1 : AT, :] = ref[AT : AT + 1, :]
        ref[AT + WIDTH : AT + WIDTH + 1, :] = ref[AT + WIDTH - 1 : AT + WIDTH, :]

    def along(src, dst):
        def strip(i):
            at = pl.multiple_of(i * STRIP, STRIP)
            block = src[pl.ds(at + AT, STRIP + 8), :]
            dst[pl.ds(at + AT, STRIP), :] = g(block[1 : STRIP + 1] - block[:STRIP])

        each(0, WIDTH // STRIP, strip)

    def smooth_tile(t):
        @pl.when(t + 1 < TILES)
        def _():
            ready(t + 1)

        s1_obs(t).wait_recv()
        s2_obs(t).wait_recv()
        ya[4, AT : AT + WIDTH, :] = soft(r[t] * inverse)

        def halo(k):
            r_k = hx[k, t] - dot3(uhs.at[k], vs[t, 0], vs[t, 1])
            ya[k, AT : AT + WIDTH, :] = weight(mh.at[k], t) * soft(r_k * inverse)

        each(0, 4, halo)
        for k in (0, 1, 4):
            rim(ya.at[k])
        for row, k in ((0, 0), (1, 1), (2, 4)):
            along(ya.at[k], fb.at[row])

        def net(row, at):
            block = fb[row, pl.ds(at, STRIP + 8), :]
            return block[8:] - block[7 : STRIP + 7]

        def pass1(i):
            at = pl.multiple_of(i * STRIP, STRIP)
            rows = pl.ds(at + AT, STRIP)
            y0, y1, y2, y3, own = [ya[k, rows, :] for k in range(5)]
            to0 = g(y0 - own)
            to1 = g(has1 * (y1 - own))
            yb[2, rows, :] = own + diffusion * (to0 + to1 + net(2, at))
            yb[0, rows, :] = y0 + diffusion * (g(has2 * (y2 - y0)) - to0 + net(0, at))
            yb[1, rows, :] = y1 + diffusion * (g(has3 * (y3 - y1)) - to1 + net(1, at))

        each(0, WIDTH // STRIP, pass1)
        rim(yb.at[2])
        along(yb.at[2], fb.at[2])

        def pass2(i):
            at = pl.multiple_of(i * STRIP, STRIP)
            rows = pl.ds(at + AT, STRIP)
            own = yb[2, rows, :]
            total = g(yb[0, rows, :] - own) + g(has1 * (yb[1, rows, :] - own)) + net(2, at)
            lay[t, pl.ds(at, STRIP), :] = level * (own + diffusion * total)

        each(0, WIDTH // STRIP, pass2)
        cloud_store(t).start()
        vio[t] = jnp.transpose(vt[t])
        v_store(t).start()

    def cloud_store(t):
        cols = pl.ds(pl.multiple_of(t * TILE, TILE), TILE)
        return pltpu.make_async_copy(lay.at[t], cloud_out.at[:, cols], out_sem.at[1 + t])

    def v_store(t):
        rows = pl.ds(pl.multiple_of(t * TILE, TILE), TILE)
        return pltpu.make_async_copy(vio.at[t], v_out.at[rows], out_sem.at[1 + TILES + t])

    for row in range(3):
        fb[row, :AT, :] = jnp.zeros((AT, TILE), f32)
    ready(0)
    each(0, TILES, smooth_tile)
    stores[0].wait()
    y_mask(iz).wait_send()
    y_pix(iz).wait_send()
    for copy in (z_mask, z_pix, s1_mask, s1_pix, s2_mask, s2_pix):
        copy.wait_send()

    def drain(i):
        y_obs(i, iz).wait_send()
        z_obs(i).wait_send()

    each(0, CHUNKS, drain)

    def close(t):
        s1_obs(t).wait_send()
        s2_obs(t).wait_send()
        cloud_store(t).wait()
        v_store(t).wait()

    each(0, TILES, close)


def per_device(observed, valid_mask, pix_factor, col_factor):
    any_space = pl.BlockSpec(memory_space=pl.ANY)
    full = pltpu.VMEM((TILES, TILE, TILE), f32)
    square = pltpu.VMEM((TILE, TILE), f32)
    pair = pltpu.VMEM((2, TILE, TILE), bf16)
    dma = pltpu.SemaphoreType.DMA
    return pl.pallas_call(
        kernel,
        out_shape=(
            jax.ShapeDtypeStruct((256, 256), f32),
            jax.ShapeDtypeStruct((2048, 256), f32),
            jax.ShapeDtypeStruct((256, 2048), f32),
        ),
        in_specs=[any_space] * 4,
        out_specs=[any_space] * 3,
        scratch_shapes=[
            full, full, full, full,
            pltpu.VMEM((TILES, 2, TILE, TILE), bf16),
            full,
            pltpu.VMEM((4, TILE, TILE), f32),
            full, full, full,
            pltpu.VMEM((256, 256), jnp.int32),
            pltpu.VMEM((4, 128, TILE), bf16),
            square, pair, pair, square, square, pair,
            pltpu.VMEM((3, TILE, TILE), f32),
            pltpu.VMEM((7, 32, TILE), f32),
            pltpu.VMEM((5, 8, 8, 128), f32),
            pltpu.VMEM((5, 16, 8, 128), f32),
            pltpu.VMEM((8, 128), f32),
            pltpu.VMEM((4, TILES, TILE, TILE), f32),
            pltpu.VMEM((4, 256, 256), jnp.int32),
            pltpu.VMEM((4, TILE, TILE), f32),
            pltpu.VMEM((4, 2, TILE, TILE), bf16),
            pltpu.VMEM((5, TILE + 16, TILE), f32),
            pltpu.VMEM((3, TILE + 16, TILE), f32),
            pltpu.VMEM((3, TILE + 16, TILE), f32),
            dma((2 * TILES + 2,)), dma((2 * TILES + 1,)),
            dma((5,)), dma((5,)), dma((5,)), dma((5,)),
            dma((2,)), dma((2,)), dma((4,)), dma((4,)),
            dma((3,)), dma((3,)), dma((7,)), dma((7,)),
            dma((7,)), dma((7,)), dma((3,)), dma((3,)), dma((4,)), dma((4,)),
            dma((CHUNKS + 2,)), dma((CHUNKS + 2,)), dma((CHUNKS + 2,)), dma((CHUNKS + 2,)),
            dma((TILES + 2,)), dma((TILES + 2,)), dma((TILES + 2,)), dma((TILES + 2,)),
        ],
        compiler_params=pltpu.CompilerParams(
            collective_id=0, has_side_effects=True, vmem_limit_bytes=60 * 1024 * 1024
        ),
        name="separate",
    )(observed, valid_mask, pix_factor, col_factor)


def solution(mesh):
    in_specs = (P("pix", "col"), P("pix", "col"), P("pix", None), P("col", None))
    out_specs = (P("pix", None), P("col", None), P("pix", "col"))
    return jax.shard_map(
        per_device, mesh=mesh, in_specs=in_specs, out_specs=out_specs, check_vma=False
    )
```

```python
import jax
import jax.numpy as jnp
from jax import lax
from jax.experimental import pallas as pl
from jax.experimental.pallas import tpu as pltpu
from jax.sharding import PartitionSpec as P

BANDS = 8
WIDTH = 256
ITERS = 2
TILE = 256
TILES = 8
CHUNKS = 16
Z_MARKS = (6, 7, 10)
AHEAD = 13

TOTAL = 67108864.0
diffusion = 0.2

f32 = jnp.float32
bf16 = jnp.bfloat16
MESH = pl.DeviceIdType.MESH


def split(x):
    hi = x.astype(bf16)
    return hi, (x - hi.astype(f32)).astype(bf16)


def left(x):
    hi, low = split(x)
    return jnp.concatenate([hi, hi, low], axis=1)


def right(x):
    hi, low = split(x)
    return jnp.concatenate([hi, low, hi], axis=0)


def mm(a, b):
    return lax.dot_general(a, b, (((1,), (0,)), ((), ())), preferred_element_type=f32)


def mm_nt(a, b):
    return lax.dot_general(a, b, (((1,), (1,)), ((), ())), preferred_element_type=f32)


def fold(x):
    part = x.reshape(x.shape[0] // 8, 8, x.shape[1]).sum(axis=0)
    return part[:, :128] + part[:, 128:]


def pack(*parts):
    rows = [jnp.sum(part, axis=0, keepdims=True) for part in parts]
    rows += [jnp.zeros((1, 128), f32)] * (4 - len(rows))
    return jnp.concatenate(rows, axis=0)


def kernel(
    obs_in, mask_in, u_in, v_in,
    u_out, v_out, cloud_out,
    r, w, c, vt, vs, hp, hsib, hf, vio, lay, mask, spread,
    u, us, uts, gp, gr, gt, gs, n1, n2, s1, s2, lev,
    hx, mh, uh, uhs, low_rank, low_shift, lev2, hw, way, ya, yb, fb,
    in_sem, out_sem, ss1, rs1, ss2, rs2, gss, grs, sibs, sibr,
    r1s, r1r, r2s, r2r, a2s, a2r, a1s, a1r, fs, fr,
    was, war, wbs, wbr, hys, hyr, hzs, hzr, h1s, h1r, h2s, h2r,
):
    p = lax.axis_index("pix")
    lo = lax.axis_index("col")
    core, h, z, x = p % 2, (p // 2) % 2, (p // 4) % 4, p // 16

    def dev(x, z, h, core, lo):
        return {"pix": ((x * 4 + z) * 2 + h) * 2 + core, "col": lo}

    i1 = (h * 2 + core) * 2 + lo
    i2 = x * 4 + z

    def peer1(d):
        j = (i1 + d) % 8
        return dev(x, z, j // 4, (j // 2) % 2, j % 2)

    def peer2(d):
        j = (i2 + d) % 16
        return dev(j // 4, j % 4, h, core, lo)

    sibling = dev(x, z, h, 1 - core, lo)
    col_pair = dev(x, z, h, core, 1 - lo)
    y_pair = dev(x, z, 1 - h, core, lo)
    z_next = peer2(17 - 2 * h)
    q1 = x + core * (z - x)
    q2 = z + core * (x - z)
    iy = 2 + (h + core) % 2
    iz = 5 - iy

    def ring1(q):
        return dev(q + core * (x - q), z + core * (q - z), h, core, lo)

    def ring2(q, h):
        return dev(x + core * (q - x), q + core * (z - q), h, core, lo)

    def rcopy(src, dst, send, recv, to):
        return pltpu.make_async_remote_copy(
            src_ref=src, dst_ref=dst, send_sem=send, recv_sem=recv, device_id=to, device_id_type=MESH
        )

    def each(low, high, step):
        def body(i, _):
            step(i)
            return 0

        lax.fori_loop(low, high, body, 0)

    barrier = pltpu.get_barrier_semaphore()
    for d in range(1, 8):
        pl.semaphore_signal(barrier, inc=1, device_id=peer1(d), device_id_type=MESH)
    for d in range(1, 16):
        pl.semaphore_signal(barrier, inc=1, device_id=peer2(d), device_id_type=MESH)

    loads = [pltpu.make_async_copy(v_in.at[pl.ds(t * TILE, TILE)], vio.at[t], in_sem.at[t]) for t in range(TILES)]
    loads.append(pltpu.make_async_copy(u_in, u, in_sem.at[TILES]))
    loads.append(pltpu.make_async_copy(mask_in, mask, in_sem.at[TILES + 1]))
    for t in range(TILES):
        loads.append(
            pltpu.make_async_copy(obs_in.at[:, pl.ds(t * TILE, TILE)], r.at[t], in_sem.at[TILES + 2 + t])
        )
    for load in loads:
        load.start()
    for part in range(4):
        date = lax.broadcasted_iota(jnp.int32, (128, TILE), 0)
        column = lax.broadcasted_iota(jnp.int32, (128, TILE), 1) + part * TILE
        gap = column - date * BANDS
        spread[part] = jnp.where((gap >= 0) & (gap < BANDS), 1.0, 0.0).astype(bf16)

    MASK, PIX = CHUNKS, CHUNKS + 1

    def chunk(i):
        return i // 2, pl.ds(pl.multiple_of((i % 2) * 128, 128), 128)

    def y_obs(i, slot):
        t, rows = chunk(i)
        cols = pl.ds(pl.multiple_of(t * TILE, TILE), TILE)
        return rcopy(obs_in.at[rows, cols], hx.at[slot, t, rows], hys.at[i], hyr.at[i], y_pair)

    def z_obs(i):
        t, rows = chunk(i)
        return rcopy(hx.at[iy, t, rows], hx.at[iz, t, rows], hzs.at[i], hzr.at[i], z_next)

    def ahead(i):
        t, rows = chunk(i)
        cols = pl.ds(pl.multiple_of(t * TILE, TILE), TILE)
        return rcopy(obs_in.at[rows, cols], way.at[i - AHEAD], was.at[i - AHEAD], war.at[i - AHEAD], peer2(15 + 2 * h))

    def across(i, slot):
        t, rows = chunk(i)
        return rcopy(way.at[i - AHEAD], hx.at[slot, t, rows], wbs.at[i - AHEAD], wbr.at[i - AHEAD], y_pair)

    def y_send(i):
        y_obs(i, iz).start()

    def z_send(i):
        y_obs(i, iy).wait_recv()
        z_obs(i).start()

    def y_mask(slot):
        return rcopy(mask_in, mh.at[slot], hys.at[MASK], hyr.at[MASK], y_pair)

    def y_pix(slot):
        return rcopy(u, uh.at[slot], hys.at[PIX], hyr.at[PIX], y_pair)

    z_mask = rcopy(mh.at[iy], mh.at[iz], hzs.at[MASK], hzr.at[MASK], z_next)
    z_pix = rcopy(uh.at[iy], uh.at[iz], hzs.at[PIX], hzr.at[PIX], z_next)
    s1_mask = rcopy(mask_in, mh.at[0], h1s.at[TILES], h1r.at[TILES], sibling)
    s1_pix = rcopy(u, uh.at[0], h1s.at[TILES + 1], h1r.at[TILES + 1], sibling)

    def s1_obs(t):
        cols = pl.ds(pl.multiple_of(t * TILE, TILE), TILE)
        return rcopy(obs_in.at[:, cols], hx.at[0, t], h1s.at[t], h1r.at[t], sibling)

    def s2_obs(t):
        return rcopy(hx.at[2, t], hx.at[1, t], h2s.at[t], h2r.at[t], sibling)

    s2_mask = rcopy(mh.at[2], mh.at[1], h2s.at[TILES], h2r.at[TILES], sibling)
    s2_pix = rcopy(uh.at[2], uh.at[1], h2s.at[TILES + 1], h2r.at[TILES + 1], sibling)

    for load in loads[: TILES]:
        load.wait()

    def turn_v(t):
        vt_t = jnp.transpose(vio[t])
        vt[t] = vt_t
        vs[t] = right(vt_t)

    each(0, TILES, turn_v)
    for load in loads[TILES:]:
        load.wait()

    def set_u(value):
        u[...] = value
        us[...] = left(value)

    set_u(u[...])

    def weight(mask_ref, t):
        dates = mask_ref[:, pl.ds(pl.multiple_of((t // 4) * 128, 128), 128)].astype(f32).astype(bf16)
        return mm(dates, spread[t % 4])

    def first(t, acc):
        w_t = weight(mask, t)
        w[t] = w_t
        r_t = w_t * (r[t] - mm(us[...], vs[t]))
        r[t] = r_t
        return acc + fold(r_t * r_t)

    zero = jnp.zeros((8, 128), f32)
    square = lax.fori_loop(0, TILES, first, zero)

    def all_reduce(k, message, between, early=lambda: None):
        s1[k, i1] = message
        for d in range(1, 8):
            rcopy(s1.at[k, i1], s1.at[k, i1], ss1.at[k], rs1.at[k], peer1(d)).start()
        whole = s1.at[k, pl.ds(0, 7)]
        done1 = rcopy(whole, whole, ss1.at[k], rs1.at[k], sibling)
        early()
        done1.wait_recv()
        total = s1[k, 0]
        for j in range(1, 8):
            total = total + s1[k, j]
        s2[k, i2] = total
        for d in range(1, 16):
            rcopy(s2.at[k, i2], s2.at[k, i2], ss2.at[k], rs2.at[k], peer2(d)).start()
        between()
        whole = s2.at[k, pl.ds(0, 15)]
        done2 = rcopy(whole, whole, ss2.at[k], rs2.at[k], ring1((q1 + 1) % 4))
        done2.wait_recv()
        total = s2[k, 0]
        for j in range(1, 16):
            total = total + s2[k, j]
        done1.wait_send()
        done2.wait_send()
        return jnp.sum(total, axis=1, keepdims=True)

    def level_from(square):
        return jnp.sqrt(jnp.maximum(square, 0.0) / TOTAL + 1e-06)

    pl.semaphore_wait(barrier, 22)

    def begin():
        each(0, 4, y_send)
        s1_mask.start()
        each(0, TILES, lambda t: s1_obs(t).start())

    each(AHEAD, CHUNKS - 1, lambda i: ahead(i).start())
    sums = all_reduce(0, pack(square), begin)
    lev[...] = jnp.broadcast_to(level_from(sums[0:1]), (8, 128))

    def cloud_store(t):
        cols = pl.ds(pl.multiple_of(t * TILE, TILE), TILE)
        return pltpu.make_async_copy(lay.at[t], cloud_out.at[:, cols], out_sem.at[1 + t])

    def v_store(t):
        rows = pl.ds(pl.multiple_of(t * TILE, TILE), TILE)
        return pltpu.make_async_copy(vio.at[t], v_out.at[rows], out_sem.at[1 + TILES + t])

    def weigh(k, t):
        hw[k, t] = weight(mh.at[k], t).astype(bf16)

    def set_halo(k):
        uhs[k] = left(uh[k])

    def cut(value, level):
        return jnp.minimum(jnp.maximum(value, -level), level)

    mine, other = 4 * core, 4 * (1 - core)

    def y_more(low, high):
        each(jnp.minimum(low, CHUNKS), jnp.minimum(high, CHUNKS), y_send)

    def iteration(it, _):
        level = lev[0:1, 0:1]
        final = it == ITERS - 1
        y0 = 4 + CHUNKS * it

        @pl.when(final)
        def _():
            y_mask(iy).wait_recv()
            z_mask.start()

        each(Z_MARKS[0] * it, 2 + (Z_MARKS[1] - 2) * it, z_send)
        copies = []
        for part in range(2):

            def grow(t, acc):
                hi, low = split(cut(r[t], level))
                v_hi = vs[t, pl.ds(part * 128, 128)]
                v_low = vs[t, pl.ds(TILE + part * 128, 128)]
                both = mm_nt(hi, jnp.concatenate([v_hi, v_low], axis=0))
                return acc + both[:, :128] + both[:, 128:] + mm_nt(low, v_hi)

            gp[part] = lax.fori_loop(0, TILES, grow, jnp.zeros((TILE, 128), f32))
            copies.append(rcopy(gp.at[part], gr.at[part], gss.at[part], grs.at[part], col_pair))
            copies[-1].start()
        each(2 + (Z_MARKS[1] - 2) * it, 4 + (Z_MARKS[2] - 4) * it, z_send)
        for copy in copies:
            copy.wait()
        g = jnp.concatenate([gp[0] + gr[0], gp[1] + gr[1]], axis=1)
        gt[...] = g
        gs[...] = left(g)

        def curve(t, acc):
            c_t = w[t] * mm(gs[...], vs[t])
            c[t] = c_t
            return acc + fold(c_t * c_t)

        bottom = lax.fori_loop(0, TILES, curve, zero)

        @pl.when(it == 0)
        def _():
            ahead(CHUNKS - 1).start()

        def mask_out():
            @pl.when(it == 0)
            def _():
                y_mask(iz).start()

        sums = all_reduce(1 + 2 * it, pack(fold(g * g) * 0.5, bottom), mask_out)
        step = sums[0:1] / sums[1:2]
        set_u(u[...] + step * gt[...])
        uts[...] = left(jnp.transpose(u[...]))

        @pl.when(final)
        def _():
            y_pix(iz).start()
            s1_pix.start()

            def cross(i):
                ahead(i).wait_recv()
                across(i, iy).start()

            each(AHEAD, CHUNKS, cross)

        y_more(y0, y0 + 3)

        def pull(t):
            r_t, ac = r[t], step * c[t]
            r[t] = r_t - ac
            hp[t] = mm(uts[...], right(cut(r_t, level) - ac))

        def order(i):
            return jnp.where(i == 0, 2, jnp.where(i == 1, 1, jnp.where(i == 2, 3, 0)))

        def hand(k, slot):
            return rcopy(hp.at[other + k], hsib.at[slot], sibs.at[slot], sibr.at[slot], sibling)

        def reduce1(d):
            return rcopy(hp.at[mine + (q1 + d) % 4], n1.at[d - 1], r1s.at[d - 1], r1r.at[d - 1], ring1((q1 + d) % 4))

        def pull_step(i):
            @pl.when(i < 4)
            def _():
                d = order(i)
                pull(other + (q2 + d) % 4)
                hand((q2 + d) % 4, d).start()
                pull(mine + (q1 + d) % 4)

            @pl.when(i >= 1)
            def _():
                d = order(i - 1)
                hand(0, d).wait_recv()
                tile = mine + (q1 + d) % 4
                hp[tile] = hp[tile] + hsib[d]

                @pl.when(i < 4)
                def _():
                    reduce1(d).start()

        each(0, 5, pull_step)

        def base(k):
            set_halo(k)

            def step(t):
                low_rank[k, t] = mm(uhs[k], vs[t])

            each(0, TILES, step)

        @pl.when(it == 0)
        def _():
            s1_mask.wait_recv()
            each(0, TILES, lambda t: weigh(0, t))

        @pl.when(final)
        def _():
            s1_pix.wait_recv()
            base(0)

            def turn(t):
                vio[t] = jnp.transpose(vt[t])

            each(0, TILES, turn)

        for d in (1, 3, 2):
            reduce1(d).wait_recv()
        tile = mine + q1
        hp[tile] = hp[tile] + n1[0] + n1[1] + n1[2]

        j2 = q2 * 2 + h

        def sub(ref, j):
            return ref.at[tile, pl.ds(pl.multiple_of(32 * j, 32), 32)]

        def reduce2(e):
            j = (j2 + e) % 8
            return rcopy(sub(hp, j), n2.at[e - 1], r2s.at[e - 1], r2r.at[e - 1], ring2(j // 2, j % 2))

        for e in range(1, 8):
            reduce2(e).start()

        @pl.when(final)
        def _():
            y_pix(iy).wait_recv()
            z_pix.start()
            z_mask.wait_recv()
            s2_mask.start()
            base(iy)
            each(0, TILES, lambda t: weigh(2, t))
            each(0, TILES, lambda t: weigh(3, t))

        each(4, jnp.where(final, 4, Z_MARKS[0] - 1), z_send)
        for e in range(1, 8):
            reduce2(e).wait_recv()
        piece = sub(hp, j2)[...]
        for e in range(7):
            piece = piece + n2[e]
        sub(hf, j2)[...] = piece
        norm = fold(piece * piece)

        def gather2(e, j):
            to = (j2 + e) % 8
            return rcopy(sub(hf, j), sub(hf, j), a2s.at[e - 1], a2r.at[e - 1], ring2(to // 2, to % 2))

        def gather1(d, k):
            return rcopy(hf.at[mine + k], hf.at[mine + k], a1s.at[d - 1], a1r.at[d - 1], ring1((q1 + d) % 4))

        def onward(j):
            for d in (2, 1, 3):
                piece = sub(hf, j)
                rcopy(piece, piece, a1s.at[d - 1], a1r.at[d - 1], ring1((q1 + d) % 4)).start()

        for e in (2, 6, 4, 1, 7, 3, 5):
            gather2(e, j2).start()
        onward(j2)
        y_more(y0 + 3, y0 + 9)
        for e in (2, 6, 4, 1, 7, 3, 5):
            j = (j2 + 8 - e) % 8
            gather2(e, j).wait_recv()
            onward(j)

        def pass_on(k, i, half):
            return rcopy(hf.at[half + k], hf.at[half + k], fs.at[i], fr.at[i], sibling)

        pass_on(q1, 0, mine).start()

        @pl.when(final)
        def _():
            z_pix.wait_recv()
            s2_pix.start()
            base(iz)
            s2_pix.wait_recv()
            base(1)
            s2_mask.wait_recv()
            each(0, TILES, lambda t: weigh(1, t))

        def shift(t, accs):
            s_t = w[t] * mm(us[...], right(hf[t]))
            c[t] = s_t
            r_t = r[t]
            a0, a1, a2 = accs
            return a0 + fold(r_t * r_t), a1 + fold(r_t * s_t), a2 + fold(s_t * s_t)

        def arrival(i):
            return jnp.where(i == 2, 3, jnp.where(i == 3, 2, i))

        def shift_other(i, accs):
            k = (q2 + 4 - arrival(i)) % 4
            pass_on(k, i, other).wait_recv()
            return shift(other + k, accs)

        def shift_step(i, accs):
            d = arrival(i)
            k = (q1 + 4 - d) % 4
            gather1(d, k).wait_recv()
            pass_on(k, i, mine).start()
            return shift_other(i - 1, shift(mine + k, accs))

        accs = lax.fori_loop(1, 4, shift_step, shift(mine + q1, (zero, zero, zero)))
        accs = shift_other(3, accs)
        for d in (1, 2, 3):
            reduce1(d).wait_send()
            gather1(d, q1).wait_send()
        for e in range(1, 8):
            reduce2(e).wait_send()
            gather2(e, j2).wait_send()
        for i in range(4):
            hand(i, i).wait_send()
            pass_on(i, i, mine).wait_send()
        def meanwhile():
            y_more(y0 + 9, y0 + 12)

            @pl.when(final)
            def _():
                each(1, 4, halo_shift)

        def halo_shift(k):
            def step(t):
                low_shift[k, t] = mm(uhs[k], right(hf[t]))

            each(0, TILES, step)

        def turn_shift(t):
            lay[t] = jnp.transpose(hf[t])

        def early():
            @pl.when(final)
            def _():
                halo_shift(0)
                each(0, TILES, turn_shift)

        @pl.when(it == 0)
        def _():
            z_send(Z_MARKS[0] - 1)

        sums = all_reduce(2 + 2 * it, pack(norm, *accs), meanwhile, early)
        step = sums[0:1] / sums[3:4]
        square = sums[1:2] - 2.0 * step * sums[2:3] + step * step * sums[3:4]
        lev[...] = jnp.broadcast_to(level_from(square), (8, 128))

        @pl.when(final)
        def _():
            each(Z_MARKS[2], AHEAD, z_send)

        def update(t):
            v_t = vt[t] + step * hf[t]
            vt[t] = v_t
            vs[t] = right(v_t)
            r[t] = r[t] - step * c[t]

            @pl.when(final)
            def _():
                vio[t] = vio[t] + step * lay[t]
                v_store(t).start()

        each(0, TILES, update)
        lev2[...] = jnp.broadcast_to(step, (8, 128))
        return 0

    lax.fori_loop(0, ITERS, iteration, 0)
    stores = [pltpu.make_async_copy(u, u_out, out_sem.at[0])]
    stores[0].start()

    level = lev[0:1, 0:1]
    step_col = lev2[0:1, 0:1]
    inverse = 1.0 / level
    last = 63
    side = 1 - 2 * core

    def flag(offset):
        row = p + offset
        return ((row >= 0) & (row <= last)).astype(f32)

    has1, has2, has3 = flag(-side), flag(2 * side), flag(-2 * side)

    def soft(scaled):
        return scaled - jnp.minimum(jnp.maximum(scaled, -1.0), 1.0)

    def g(e):
        return e / (1.0 + e * e)

    def arrived(i):
        @pl.when(i < AHEAD)
        def _():
            z_obs(i).wait_recv()

        @pl.when(i >= AHEAD)
        def _():
            y_obs(i, iy).wait_recv()
            across(i, iz).wait_recv()

    def ready(t):
        each(2 * t, 2 * t + 2, arrived)
        s2_obs(t).start()

    STRIP = 32
    AT = 8

    def rim(ref):
        ref[AT - 1 : AT, :] = ref[AT : AT + 1, :]
        ref[AT + WIDTH : AT + WIDTH + 1, :] = ref[AT + WIDTH - 1 : AT + WIDTH, :]

    def along(src, dst):
        for at in range(AT, AT + WIDTH, STRIP):
            dst[pl.ds(at, STRIP), :] = g(src[pl.ds(at + 1, STRIP), :] - src[pl.ds(at, STRIP), :])

    def smooth_tile(t):
        @pl.when(t + 1 < TILES)
        def _():
            ready(t + 1)

        s1_obs(t).wait_recv()
        s2_obs(t).wait_recv()

        def halo(k, at):
            rows = pl.ds(at, STRIP)
            r_k = hx[k, t, rows, :] - low_rank[k, t, rows, :] - step_col * low_shift[k, t, rows, :]
            return hw[k, t, rows, :].astype(f32) * soft(r_k * inverse)

        for at in range(0, WIDTH, STRIP):
            rows = pl.ds(at + AT, STRIP)
            ya[2, rows, :] = soft(r[t, pl.ds(at, STRIP), :] * inverse)
            ya[0, rows, :] = halo(0, at)
            ya[1, rows, :] = halo(1, at)
        for row in range(3):
            rim(ya.at[row])
            along(ya.at[row], fb.at[row])

        def net(row, at):
            return fb[row, pl.ds(at + AT, STRIP), :] - fb[row, pl.ds(at + AT - 1, STRIP), :]

        for at in range(0, WIDTH, STRIP):
            rows = pl.ds(at + AT, STRIP)
            y0, y1, own = [ya[k, rows, :] for k in range(3)]
            to0 = g(y0 - own)
            to1 = g(has1 * (y1 - own))
            yb[2, rows, :] = own + diffusion * (to0 + to1 + net(2, at))
            yb[0, rows, :] = y0 + diffusion * (g(has2 * (halo(2, at) - y0)) - to0 + net(0, at))
            yb[1, rows, :] = y1 + diffusion * (g(has3 * (halo(3, at) - y1)) - to1 + net(1, at))
        rim(yb.at[2])
        along(yb.at[2], fb.at[2])
        for at in range(0, WIDTH, STRIP):
            rows = pl.ds(at + AT, STRIP)
            own = yb[2, rows, :]
            total = g(yb[0, rows, :] - own) + g(has1 * (yb[1, rows, :] - own)) + net(2, at)
            lay[t, pl.ds(at, STRIP), :] = level * (own + diffusion * total)
        cloud_store(t).start()

    for row in range(3):
        fb[row, :AT, :] = jnp.zeros((AT, TILE), f32)
    ready(0)
    each(0, TILES, smooth_tile)
    stores[0].wait()
    y_mask(iz).wait_send()
    y_pix(iz).wait_send()
    for copy in (z_mask, z_pix, s1_mask, s1_pix, s2_mask, s2_pix):
        copy.wait_send()

    def drain(i):
        y_obs(i, iz).wait_send()

        @pl.when(i < AHEAD)
        def _():
            z_obs(i).wait_send()

        @pl.when(i >= AHEAD)
        def _():
            ahead(i).wait_send()
            across(i, iy).wait_send()

    each(0, CHUNKS, drain)

    def close(t):
        s1_obs(t).wait_send()
        s2_obs(t).wait_send()
        cloud_store(t).wait()
        v_store(t).wait()

    each(0, TILES, close)


def hand_out(u_in, v_in, c_in, u_out, v_out, c_out, ub, vb, cb, load_sem, store_sem):
    moves = [(u_in, ub, u_out)]
    for i in range(4):
        rows = pl.ds(512 * i, 512)
        moves.append((v_in.at[rows], vb.at[rows], v_out.at[rows]))
        rows = pl.ds(64 * i, 64)
        moves.append((c_in.at[rows], cb.at[rows], c_out.at[rows]))
    loads = [pltpu.make_async_copy(a, b, load_sem.at[i]) for i, (a, b, _) in enumerate(moves)]
    stores = [pltpu.make_async_copy(b, c, store_sem.at[i]) for i, (_, b, c) in enumerate(moves)]
    for load in loads:
        load.start()
    for load, store in zip(loads, stores):
        load.wait()
        store.start()
    for store in stores:
        store.wait()


def per_device(observed, valid_mask, pix_factor, col_factor):
    any_space = pl.BlockSpec(memory_space=pl.ANY)
    full = pltpu.VMEM((TILES, TILE, TILE), f32)
    square = pltpu.VMEM((TILE, TILE), f32)
    pair = pltpu.VMEM((TILE, 3 * TILE), bf16)
    dma = pltpu.SemaphoreType.DMA
    shapes = (
        jax.ShapeDtypeStruct((256, 256), f32),
        jax.ShapeDtypeStruct((2048, 256), f32),
        jax.ShapeDtypeStruct((256, 2048), f32),
    )
    results = pl.pallas_call(
        kernel,
        out_shape=shapes,
        in_specs=[any_space] * 4,
        out_specs=[any_space] * 3,
        scratch_shapes=[
            full, full, full, full,
            pltpu.VMEM((TILES, 3 * TILE, TILE), bf16),
            full,
            pltpu.VMEM((4, TILE, TILE), f32),
            full, full, full,
            pltpu.VMEM((256, 256), jnp.int32),
            pltpu.VMEM((4, 128, TILE), bf16),
            square, pair, pair,
            pltpu.VMEM((2, TILE, 128), f32), pltpu.VMEM((2, TILE, 128), f32),
            square, pair,
            pltpu.VMEM((3, TILE, TILE), f32),
            pltpu.VMEM((7, 32, TILE), f32),
            pltpu.VMEM((5, 8, 4, 128), f32),
            pltpu.VMEM((5, 16, 4, 128), f32),
            pltpu.VMEM((8, 128), f32),
            pltpu.VMEM((4, TILES, TILE, TILE), f32),
            pltpu.VMEM((4, 256, 256), jnp.int32),
            pltpu.VMEM((4, TILE, TILE), f32),
            pltpu.VMEM((4, TILE, 3 * TILE), bf16),
            pltpu.VMEM((4, TILES, TILE, TILE), f32),
            pltpu.VMEM((4, TILES, TILE, TILE), f32),
            pltpu.VMEM((8, 128), f32),
            pltpu.VMEM((4, TILES, TILE, TILE), bf16),
            pltpu.VMEM((CHUNKS - AHEAD, 128, TILE), f32),
            pltpu.VMEM((3, TILE + 16, TILE), f32),
            pltpu.VMEM((3, TILE + 16, TILE), f32),
            pltpu.VMEM((3, TILE + 16, TILE), f32),
            dma((2 * TILES + 2,)), dma((2 * TILES + 1,)),
            dma((5,)), dma((5,)), dma((5,)), dma((5,)),
            dma((2,)), dma((2,)), dma((4,)), dma((4,)),
            dma((3,)), dma((3,)), dma((7,)), dma((7,)),
            dma((7,)), dma((7,)), dma((3,)), dma((3,)), dma((4,)), dma((4,)),
            dma((3,)), dma((3,)), dma((3,)), dma((3,)),
            dma((CHUNKS + 2,)), dma((CHUNKS + 2,)), dma((CHUNKS + 2,)), dma((CHUNKS + 2,)),
            dma((TILES + 2,)), dma((TILES + 2,)), dma((TILES + 2,)), dma((TILES + 2,)),
        ],
        compiler_params=pltpu.CompilerParams(
            collective_id=0, has_side_effects=True, vmem_limit_bytes=60 * 1024 * 1024
        ),
        name="separate",
    )(observed, valid_mask, pix_factor, col_factor)
    return pl.pallas_call(
        hand_out,
        out_shape=shapes,
        in_specs=[any_space] * 3,
        out_specs=[any_space] * 3,
        scratch_shapes=[
            square,
            pltpu.VMEM((2048, 256), f32),
            pltpu.VMEM((256, 2048), f32),
            dma((9,)), dma((9,)),
        ],
        compiler_params=pltpu.CompilerParams(vmem_limit_bytes=60 * 1024 * 1024),
        name="hand_out",
    )(*results)


def solution(mesh):
    in_specs = (P("pix", "col"), P("pix", "col"), P("pix", None), P("col", None))
    out_specs = (P("pix", None), P("col", None), P("pix", "col"))
    return jax.shard_map(
        per_device, mesh=mesh, in_specs=in_specs, out_specs=out_specs, check_vma=False
    )
```

```python
import jax
import jax.numpy as jnp
from jax import lax
from jax.experimental import pallas as pl
from jax.experimental.pallas import tpu as pltpu
from jax.sharding import PartitionSpec as P

BANDS = 8
WIDTH = 256
ITERS = 2
TILE = 256
TILES = 8
CHUNKS = 16
Z_MARKS = (5, 6, 9)
AHEAD = 11

TOTAL = 67108864.0
diffusion = 0.2

f32 = jnp.float32
bf16 = jnp.bfloat16
MESH = pl.DeviceIdType.MESH


def split(x):
    hi = x.astype(bf16)
    return hi, (x - hi.astype(f32)).astype(bf16)


def left(x):
    hi, low = split(x)
    return jnp.concatenate([hi, hi, low], axis=1)


def right(x):
    hi, low = split(x)
    return jnp.concatenate([hi, low, hi], axis=0)


def mm(a, b):
    return lax.dot_general(a, b, (((1,), (0,)), ((), ())), preferred_element_type=f32)


def mm_nt(a, b):
    return lax.dot_general(a, b, (((1,), (1,)), ((), ())), preferred_element_type=f32)


def fold(x):
    part = x.reshape(x.shape[0] // 8, 8, x.shape[1]).sum(axis=0)
    return part[:, :128] + part[:, 128:]


def pack(*parts):
    rows = [jnp.sum(part, axis=0, keepdims=True) for part in parts]
    rows += [jnp.zeros((1, 128), f32)] * (4 - len(rows))
    return jnp.concatenate(rows, axis=0)


def kernel(
    obs_in, mask_in, u_in, v_in,
    u_out, vio, lay,
    r, w, c, vt, vs, hp, hsib, hf, mask, spread,
    u, us, uts, gp, gr, gt, gs, n1, n2, s1, s2, lev,
    hx, mh, uh, uhs, low_rank, low_shift, lev2, hw, way, ya, yb, yc, y_sib, p_sib, p_far, fb,
    in_sem, ss1, rs1, ss2, rs2, gss, grs, sibs, sibr,
    r1s, r1r, r2s, r2r, a2s, a2r, a1s, a1r, fs, fr,
    was, war, wbs, wbr, hys, hyr, hzs, hzr, h1s, h1r, h2s, h2r,
):
    p = lax.axis_index("pix")
    lo = lax.axis_index("col")
    core, h, z, x = p % 2, (p // 2) % 2, (p // 4) % 4, p // 16

    def dev(x, z, h, core, lo):
        return {"pix": ((x * 4 + z) * 2 + h) * 2 + core, "col": lo}

    i1 = (h * 2 + core) * 2 + lo
    i2 = x * 4 + z

    def peer1(d):
        j = (i1 + d) % 8
        return dev(x, z, j // 4, (j // 2) % 2, j % 2)

    def peer2(d):
        j = (i2 + d) % 16
        return dev(j // 4, j % 4, h, core, lo)

    sibling = dev(x, z, h, 1 - core, lo)
    col_pair = dev(x, z, h, core, 1 - lo)
    y_pair = dev(x, z, 1 - h, core, lo)
    z_next = peer2(17 - 2 * h)
    q1 = x + core * (z - x)
    q2 = z + core * (x - z)
    iy = 1 + (h + core) % 2
    iz = 3 - iy

    def ring1(q):
        return dev(q + core * (x - q), z + core * (q - z), h, core, lo)

    def ring2(q, h):
        return dev(x + core * (q - x), q + core * (z - q), h, core, lo)

    def rcopy(src, dst, send, recv, to):
        return pltpu.make_async_remote_copy(
            src_ref=src, dst_ref=dst, send_sem=send, recv_sem=recv, device_id=to, device_id_type=MESH
        )

    def each(low, high, step):
        def body(i, _):
            step(i)
            return 0

        lax.fori_loop(low, high, body, 0)

    barrier = pltpu.get_barrier_semaphore()
    for d in range(1, 8):
        pl.semaphore_signal(barrier, inc=1, device_id=peer1(d), device_id_type=MESH)
    for d in range(1, 16):
        pl.semaphore_signal(barrier, inc=1, device_id=peer2(d), device_id_type=MESH)

    loads = [pltpu.make_async_copy(v_in.at[pl.ds(t * TILE, TILE)], vio.at[t], in_sem.at[t]) for t in range(TILES)]
    loads.append(pltpu.make_async_copy(u_in, u, in_sem.at[TILES]))
    loads.append(pltpu.make_async_copy(mask_in, mask, in_sem.at[TILES + 1]))
    for t in range(TILES):
        loads.append(
            pltpu.make_async_copy(obs_in.at[:, pl.ds(t * TILE, TILE)], r.at[t], in_sem.at[TILES + 2 + t])
        )
    for load in loads:
        load.start()
    for part in range(4):
        date = lax.broadcasted_iota(jnp.int32, (128, TILE), 0)
        column = lax.broadcasted_iota(jnp.int32, (128, TILE), 1) + part * TILE
        gap = column - date * BANDS
        spread[part] = jnp.where((gap >= 0) & (gap < BANDS), 1.0, 0.0).astype(bf16)

    MASK, PIX = CHUNKS, CHUNKS + 1

    def chunk(i):
        return i // 2, pl.ds(pl.multiple_of((i % 2) * 128, 128), 128)

    def y_obs(i, slot):
        t, rows = chunk(i)
        cols = pl.ds(pl.multiple_of(t * TILE, TILE), TILE)
        return rcopy(obs_in.at[rows, cols], hx.at[slot, t, rows], hys.at[i], hyr.at[i], y_pair)

    def z_obs(i):
        t, rows = chunk(i)
        return rcopy(hx.at[iy, t, rows], hx.at[iz, t, rows], hzs.at[i], hzr.at[i], z_next)

    def ahead(i):
        t, rows = chunk(i)
        cols = pl.ds(pl.multiple_of(t * TILE, TILE), TILE)
        return rcopy(obs_in.at[rows, cols], way.at[i - AHEAD], was.at[i - AHEAD], war.at[i - AHEAD], peer2(15 + 2 * h))

    def across(i, slot):
        t, rows = chunk(i)
        return rcopy(way.at[i - AHEAD], hx.at[slot, t, rows], wbs.at[i - AHEAD], wbr.at[i - AHEAD], y_pair)

    def y_send(i):
        y_obs(i, iz).start()

    def z_send(i):
        y_obs(i, iy).wait_recv()
        z_obs(i).start()

    def y_mask(slot):
        return rcopy(mask_in, mh.at[slot], hys.at[MASK], hyr.at[MASK], y_pair)

    def y_pix(slot):
        return rcopy(u, uh.at[slot], hys.at[PIX], hyr.at[PIX], y_pair)

    z_mask = rcopy(mh.at[iy], mh.at[iz], hzs.at[MASK], hzr.at[MASK], z_next)
    z_pix = rcopy(uh.at[iy], uh.at[iz], hzs.at[PIX], hzr.at[PIX], z_next)
    AT = 8
    inner = pl.ds(AT, WIDTH)

    def s1_layer(t):
        return rcopy(ya.at[t, inner], y_sib.at[t], h1s.at[t], h1r.at[t], sibling)

    def s1_pass(t):
        return rcopy(yb.at[t, inner], p_sib.at[t], h1s.at[TILES + t], h1r.at[TILES + t], sibling)

    def s2_obs(t):
        return rcopy(hx.at[1, t], hx.at[0, t], h2s.at[t], h2r.at[t], sibling)

    s2_mask = rcopy(mh.at[1], mh.at[0], h2s.at[TILES], h2r.at[TILES], sibling)
    s2_pix = rcopy(uh.at[1], uh.at[0], h2s.at[TILES + 1], h2r.at[TILES + 1], sibling)

    for load in loads[: TILES]:
        load.wait()

    def turn_v(t):
        vt_t = jnp.transpose(vio[t])
        vt[t] = vt_t
        vs[t] = right(vt_t)

    each(0, TILES, turn_v)
    for load in loads[TILES:]:
        load.wait()

    def set_u(value):
        u[...] = value
        us[...] = left(value)

    set_u(u[...])

    def weight(mask_ref, t):
        dates = mask_ref[:, pl.ds(pl.multiple_of((t // 4) * 128, 128), 128)].astype(f32).astype(bf16)
        return mm(dates, spread[t % 4])

    def first(t, acc):
        w_t = weight(mask, t)
        w[t] = w_t
        r_t = w_t * (r[t] - mm(us[...], vs[t]))
        r[t] = r_t
        return acc + fold(r_t * r_t)

    zero = jnp.zeros((8, 128), f32)
    square = lax.fori_loop(0, TILES, first, zero)

    def arrived(i):
        @pl.when(i < AHEAD)
        def _():
            z_obs(i).wait_recv()

        @pl.when(i >= AHEAD)
        def _():
            y_obs(i, iy).wait_recv()
            across(i, iz).wait_recv()

    def ready(t):
        each(2 * t, 2 * t + 2, arrived)
        s2_obs(t).start()

    def turn_of(i):
        return (i + 6) % TILES

    def all_reduce(k, message, between, early=lambda: None):
        s1[k, i1] = message
        for d in range(1, 8):
            rcopy(s1.at[k, i1], s1.at[k, i1], ss1.at[k], rs1.at[k], peer1(d)).start()
        whole = s1.at[k, pl.ds(0, 7)]
        done1 = rcopy(whole, whole, ss1.at[k], rs1.at[k], sibling)
        early()
        done1.wait_recv()
        total = s1[k, 0]
        for j in range(1, 8):
            total = total + s1[k, j]
        s2[k, i2] = total
        for d in range(1, 16):
            rcopy(s2.at[k, i2], s2.at[k, i2], ss2.at[k], rs2.at[k], peer2(d)).start()
        between()
        whole = s2.at[k, pl.ds(0, 15)]
        done2 = rcopy(whole, whole, ss2.at[k], rs2.at[k], ring1((q1 + 1) % 4))
        done2.wait_recv()
        total = s2[k, 0]
        for j in range(1, 16):
            total = total + s2[k, j]
        done1.wait_send()
        done2.wait_send()
        return jnp.sum(total, axis=1, keepdims=True)

    def level_from(square):
        return jnp.sqrt(jnp.maximum(square, 0.0) / TOTAL + 1e-06)

    pl.semaphore_wait(barrier, 22)

    def begin():
        each(0, 3, y_send)

    each(AHEAD, CHUNKS - 2, lambda i: ahead(i).start())
    sums = all_reduce(0, pack(square), begin)
    lev[...] = jnp.broadcast_to(level_from(sums[0:1]), (8, 128))

    def soft(scaled):
        return scaled - jnp.minimum(jnp.maximum(scaled, -1.0), 1.0)

    def weigh(k, t):
        hw[k // 2, t] = weight(mh.at[k], t).astype(bf16)

    def set_halo(k):
        uhs[k // 2] = left(uh[k])

    def cut(value, level):
        return jnp.minimum(jnp.maximum(value, -level), level)

    mine, other = 4 * core, 4 * (1 - core)

    def y_more(low, high):
        each(jnp.minimum(low, CHUNKS), jnp.minimum(high, CHUNKS), y_send)

    def iteration(it, _):
        level = lev[0:1, 0:1]
        final = it == ITERS - 1
        y0 = 3 + CHUNKS * it

        @pl.when(final)
        def _():
            y_mask(iy).wait_recv()
            z_mask.start()

        @pl.when(it == 0)
        def _():
            ahead(CHUNKS - 2).start()

        each(Z_MARKS[0] * it, 2 + (Z_MARKS[1] - 2) * it, z_send)
        copies = []
        for part in range(2):

            def grow(t, acc):
                hi, low = split(cut(r[t], level))
                v_hi = vs[t, pl.ds(part * 128, 128)]
                v_low = vs[t, pl.ds(TILE + part * 128, 128)]
                both = mm_nt(hi, jnp.concatenate([v_hi, v_low], axis=0))
                return acc + both[:, :128] + both[:, 128:] + mm_nt(low, v_hi)

            gp[part] = lax.fori_loop(0, TILES, grow, jnp.zeros((TILE, 128), f32))
            copies.append(rcopy(gp.at[part], gr.at[part], gss.at[part], grs.at[part], col_pair))
            copies[-1].start()
        each(2 + (Z_MARKS[1] - 2) * it, 3 + (Z_MARKS[2] - 3) * it, z_send)
        for copy in copies:
            copy.wait()
        g = jnp.concatenate([gp[0] + gr[0], gp[1] + gr[1]], axis=1)
        gt[...] = g
        gs[...] = left(g)

        def curve(t, acc):
            c_t = w[t] * mm(gs[...], vs[t])
            c[t] = c_t
            return acc + fold(c_t * c_t)

        bottom = lax.fori_loop(0, TILES, curve, zero)

        @pl.when(it == 0)
        def _():
            ahead(CHUNKS - 1).start()

        def cross(i):
            ahead(i).wait_recv()
            across(i, iy).start()

        def mask_out():
            @pl.when(it == 0)
            def _():
                y_mask(iz).start()

            @pl.when(final)
            def _():
                each(AHEAD, AHEAD + 2, cross)

        sums = all_reduce(1 + 2 * it, pack(fold(g * g) * 0.5, bottom), mask_out)
        step = sums[0:1] / sums[1:2]
        set_u(u[...] + step * gt[...])
        uts[...] = left(jnp.transpose(u[...]))

        @pl.when(final)
        def _():
            y_pix(iz).start()

        y_more(y0, y0 + 4)

        def pull(t):
            r_t, ac = r[t], step * c[t]
            r[t] = r_t - ac
            hp[t] = mm(uts[...], right(cut(r_t, level) - ac))

        def order(i):
            return jnp.where(i == 0, 2, jnp.where(i == 1, 1, jnp.where(i == 2, 3, 0)))

        def hand(k, slot):
            return rcopy(hp.at[other + k], hsib.at[slot], sibs.at[slot], sibr.at[slot], sibling)

        def reduce1(d):
            return rcopy(hp.at[mine + (q1 + d) % 4], n1.at[d - 1], r1s.at[d - 1], r1r.at[d - 1], ring1((q1 + d) % 4))

        def pull_step(i):
            @pl.when(i < 4)
            def _():
                d = order(i)
                pull(other + (q2 + d) % 4)
                hand((q2 + d) % 4, d).start()
                pull(mine + (q1 + d) % 4)

            @pl.when(i >= 1)
            def _():
                d = order(i - 1)
                hand(0, d).wait_recv()
                tile = mine + (q1 + d) % 4
                hp[tile] = hp[tile] + hsib[d]

                @pl.when(i < 4)
                def _():
                    reduce1(d).start()

        each(0, 5, pull_step)

        def base(k):
            set_halo(k)

            def step(t):
                low_rank[k // 2, t] = mm(uhs[k // 2], vs[t])

            each(0, TILES, step)

        @pl.when(final)
        def _():
            def turn(t):
                vio[t] = jnp.transpose(vt[t])

            each(0, TILES, turn)

        for d in (1, 3, 2):
            reduce1(d).wait_recv()
        tile = mine + q1
        hp[tile] = hp[tile] + n1[0] + n1[1] + n1[2]

        j2 = q2 * 2 + h

        def sub(ref, j):
            return ref.at[tile, pl.ds(pl.multiple_of(32 * j, 32), 32)]

        def reduce2(e):
            j = (j2 + e) % 8
            return rcopy(sub(hp, j), n2.at[e - 1], r2s.at[e - 1], r2r.at[e - 1], ring2(j // 2, j % 2))

        for e in range(1, 8):
            reduce2(e).start()

        @pl.when(final)
        def _():
            y_pix(iy).wait_recv()
            z_pix.start()
            z_mask.wait_recv()
            s2_mask.start()
            each(0, TILES, lambda t: weigh(2, t))

            @pl.when(iy == 1)
            def _():
                s2_pix.start()

            @pl.when(iy == 2)
            def _():
                base(2)

            s2_mask.wait_recv()
            each(0, TILES, lambda t: weigh(0, t))

        each(3, jnp.where(final, 3, Z_MARKS[0] - 1), z_send)
        for e in range(1, 8):
            reduce2(e).wait_recv()
        piece = sub(hp, j2)[...]
        for e in range(7):
            piece = piece + n2[e]
        sub(hf, j2)[...] = piece
        norm = fold(piece * piece)

        def gather2(e, j):
            to = (j2 + e) % 8
            return rcopy(sub(hf, j), sub(hf, j), a2s.at[e - 1], a2r.at[e - 1], ring2(to // 2, to % 2))

        def gather1(d, k):
            return rcopy(hf.at[mine + k], hf.at[mine + k], a1s.at[d - 1], a1r.at[d - 1], ring1((q1 + d) % 4))

        def onward(j):
            for d in (2, 1, 3):
                piece = sub(hf, j)
                rcopy(piece, piece, a1s.at[d - 1], a1r.at[d - 1], ring1((q1 + d) % 4)).start()

        for e in (2, 6, 4, 1, 7, 3, 5):
            gather2(e, j2).start()
        onward(j2)
        y_more(y0 + 4, y0 + 10)

        @pl.when(final)
        def _():
            each(AHEAD + 2, CHUNKS, cross)

        for e in (2, 6, 4, 1, 7, 3, 5):
            j = (j2 + 8 - e) % 8
            gather2(e, j).wait_recv()
            onward(j)

        def pass_on(k, i, half):
            return rcopy(hf.at[half + k], hf.at[half + k], fs.at[i], fr.at[i], sibling)

        pass_on(q1, 0, mine).start()

        @pl.when(final)
        def _():
            z_pix.wait_recv()

            @pl.when(iy == 2)
            def _():
                s2_pix.start()

            @pl.when(iy == 1)
            def _():
                base(2)

            s2_pix.wait_recv()
            base(0)

        def shift(t, accs):
            s_t = w[t] * mm(us[...], right(hf[t]))
            c[t] = s_t
            r_t = r[t]
            a0, a1, a2 = accs
            return a0 + fold(r_t * r_t), a1 + fold(r_t * s_t), a2 + fold(s_t * s_t)

        def arrival(i):
            return jnp.where(i == 2, 3, jnp.where(i == 3, 2, i))

        def shift_other(i, accs):
            k = (q2 + 4 - arrival(i)) % 4
            pass_on(k, i, other).wait_recv()
            return shift(other + k, accs)

        def shift_step(i, accs):
            d = arrival(i)
            k = (q1 + 4 - d) % 4
            gather1(d, k).wait_recv()
            pass_on(k, i, mine).start()
            return shift_other(i - 1, shift(mine + k, accs))

        accs = lax.fori_loop(1, 4, shift_step, shift(mine + q1, (zero, zero, zero)))
        accs = shift_other(3, accs)
        for d in (1, 2, 3):
            reduce1(d).wait_send()
            gather1(d, q1).wait_send()
        for e in range(1, 8):
            reduce2(e).wait_send()
            gather2(e, j2).wait_send()
        for i in range(4):
            hand(i, i).wait_send()
            pass_on(i, i, mine).wait_send()
        def meanwhile():
            y_more(y0 + 10, y0 + 13)

            @pl.when(final)
            def _():
                each(0, 2, halo_shift)
                ready(turn_of(0))
                ready(turn_of(1))

        def halo_shift(k):
            def step(t):
                low_shift[k, t] = mm(uhs[k], right(hf[t]))

            each(0, TILES, step)

        def turn_shift(t):
            lay[t] = jnp.transpose(hf[t])

        def early():
            @pl.when(final)
            def _():
                each(0, TILES, turn_shift)

        @pl.when(it == 0)
        def _():
            z_send(Z_MARKS[0] - 1)

        sums = all_reduce(2 + 2 * it, pack(norm, *accs), meanwhile, early)
        step = sums[0:1] / sums[3:4]
        square = sums[1:2] - 2.0 * step * sums[2:3] + step * step * sums[3:4]
        lev[...] = jnp.broadcast_to(level_from(square), (8, 128))

        @pl.when(final)
        def _():
            each(Z_MARKS[2], AHEAD, z_send)

        inverse = 1.0 / level_from(square)

        def update(t):
            v_t = vt[t] + step * hf[t]
            vt[t] = v_t
            vs[t] = right(v_t)
            r_t = r[t] - step * c[t]
            r[t] = r_t

            @pl.when(final)
            def _():
                ya[t, inner, :] = soft(r_t * inverse)
                s1_layer(t).start()
                vio[t] = vio[t] + step * lay[t]

        each(0, TILES, update)
        lev2[...] = jnp.broadcast_to(step, (8, 128))
        return 0

    lax.fori_loop(0, ITERS, iteration, 0)
    u_out[...] = u[...]

    level = lev[0:1, 0:1]
    step_col = lev2[0:1, 0:1]
    inverse = 1.0 / level
    last = 63
    side = 1 - 2 * core

    def flag(offset):
        row = p + offset
        return ((row >= 0) & (row <= last)).astype(f32)

    has1, has2 = flag(-side), flag(-2 * side)

    def g(e):
        return e / (1.0 + e * e)

    STRIP = 32
    strips = range(0, WIDTH, STRIP)

    def rim(ref):
        ref[AT - 1 : AT, :] = ref[AT : AT + 1, :]
        ref[AT + WIDTH : AT + WIDTH + 1, :] = ref[AT + WIDTH - 1 : AT + WIDTH, :]

    def along(src, dst):
        rim(src)
        for at in range(AT, AT + WIDTH, STRIP):
            dst[pl.ds(at, STRIP), :] = g(src[pl.ds(at + 1, STRIP), :] - src[pl.ds(at, STRIP), :])

    def net(row, at):
        return fb[row, pl.ds(at + AT, STRIP), :] - fb[row, pl.ds(at + AT - 1, STRIP), :]

    def pass1(t):
        s2_obs(t).wait_recv()

        def halo(k, at):
            rows = pl.ds(at, STRIP)
            r_k = hx[2 * k, t, rows, :] - low_rank[k, t, rows, :] - step_col * low_shift[k, t, rows, :]
            return hw[k, t, rows, :].astype(f32) * soft(r_k * inverse)

        for at in strips:
            yc[pl.ds(at + AT, STRIP), :] = halo(0, at)
        along(ya.at[t], fb.at[0])
        along(yc, fb.at[1])
        s1_layer(t).wait_recv()
        for at in strips:
            rows = pl.ds(at + AT, STRIP)
            own, y1 = ya[t, rows, :], yc[rows, :]
            to1 = g(has1 * (y1 - own))
            yb[t, rows, :] = own + diffusion * (g(y_sib[t, pl.ds(at, STRIP), :] - own) + to1 + net(0, at))
            p_far[t, pl.ds(at, STRIP), :] = y1 + diffusion * (g(has2 * (halo(1, at) - y1)) - to1 + net(1, at))
        s1_pass(t).start()

    def pass2(t):
        along(yb.at[t], fb.at[2])
        s1_pass(t).wait_recv()
        for at in strips:
            rows = pl.ds(at, STRIP)
            own = yb[t, pl.ds(at + AT, STRIP), :]
            total = g(p_sib[t, rows, :] - own) + g(has1 * (p_far[t, rows, :] - own)) + net(2, at)
            lay[t, rows, :] = level * (own + diffusion * total)

    def smooth_tile(i):
        @pl.when(i < TILES)
        def _():
            @pl.when(i + 2 < TILES)
            def _():
                ready(turn_of(i + 2))

            pass1(turn_of(i))

        @pl.when(i > 1)
        def _():
            pass2(turn_of(i - 2))

    for row in range(3):
        fb[row, :AT, :] = jnp.zeros((AT, TILE), f32)
    each(0, TILES + 2, smooth_tile)
    y_mask(iz).wait_send()
    y_pix(iz).wait_send()
    for copy in (z_mask, z_pix, s2_mask, s2_pix):
        copy.wait_send()

    def drain(i):
        y_obs(i, iz).wait_send()

        @pl.when(i < AHEAD)
        def _():
            z_obs(i).wait_send()

        @pl.when(i >= AHEAD)
        def _():
            ahead(i).wait_send()
            across(i, iy).wait_send()

    each(0, CHUNKS, drain)

    def close(t):
        s1_layer(t).wait_send()
        s1_pass(t).wait_send()
        s2_obs(t).wait_send()

    each(0, TILES, close)


def hand_out(u_in, v_in, c_in, u_out, v_out, c_out, sem):
    moves = [(u_in, u_out)]
    for t in range(TILES):
        span = pl.ds(t * TILE, TILE)
        moves += [(v_in.at[t], v_out.at[span]), (c_in.at[t], c_out.at[:, span])]
    stores = [pltpu.make_async_copy(a, b, sem.at[i]) for i, (a, b) in enumerate(moves)]
    for store in stores:
        store.start()
    for store in stores:
        store.wait()


def per_device(observed, valid_mask, pix_factor, col_factor):
    any_space = pl.BlockSpec(memory_space=pl.ANY)
    full = pltpu.VMEM((TILES, TILE, TILE), f32)
    square = pltpu.VMEM((TILE, TILE), f32)
    pair = pltpu.VMEM((TILE, 3 * TILE), bf16)
    dma = pltpu.SemaphoreType.DMA
    shapes = (
        jax.ShapeDtypeStruct((256, 256), f32),
        jax.ShapeDtypeStruct((2048, 256), f32),
        jax.ShapeDtypeStruct((256, 2048), f32),
    )
    results = pl.pallas_call(
        kernel,
        out_shape=(
            pltpu.VMEM((TILE, TILE), f32),
            pltpu.VMEM((TILES, TILE, TILE), f32),
            pltpu.VMEM((TILES, TILE, TILE), f32),
        ),
        in_specs=[any_space] * 4,
        out_specs=[pl.BlockSpec(memory_space=pltpu.VMEM)] * 3,
        scratch_shapes=[
            full, full, full, full,
            pltpu.VMEM((TILES, 3 * TILE, TILE), bf16),
            full,
            pltpu.VMEM((4, TILE, TILE), f32),
            full,
            pltpu.VMEM((256, 256), jnp.int32),
            pltpu.VMEM((4, 128, TILE), bf16),
            square, pair, pair,
            pltpu.VMEM((2, TILE, 128), f32), pltpu.VMEM((2, TILE, 128), f32),
            square, pair,
            pltpu.VMEM((3, TILE, TILE), f32),
            pltpu.VMEM((7, 32, TILE), f32),
            pltpu.VMEM((5, 8, 4, 128), f32),
            pltpu.VMEM((5, 16, 4, 128), f32),
            pltpu.VMEM((8, 128), f32),
            pltpu.VMEM((3, TILES, TILE, TILE), f32),
            pltpu.VMEM((3, 256, 256), jnp.int32),
            pltpu.VMEM((3, TILE, TILE), f32),
            pltpu.VMEM((2, TILE, 3 * TILE), bf16),
            pltpu.VMEM((2, TILES, TILE, TILE), f32),
            pltpu.VMEM((2, TILES, TILE, TILE), f32),
            pltpu.VMEM((8, 128), f32),
            pltpu.VMEM((2, TILES, TILE, TILE), bf16),
            pltpu.VMEM((CHUNKS - AHEAD, 128, TILE), f32),
            pltpu.VMEM((TILES, TILE + 16, TILE), f32),
            pltpu.VMEM((TILES, TILE + 16, TILE), f32),
            pltpu.VMEM((TILE + 16, TILE), f32),
            full, full,
            full,
            pltpu.VMEM((3, TILE + 16, TILE), f32),
            dma((2 * TILES + 2,)),
            dma((5,)), dma((5,)), dma((5,)), dma((5,)),
            dma((2,)), dma((2,)), dma((4,)), dma((4,)),
            dma((3,)), dma((3,)), dma((7,)), dma((7,)),
            dma((7,)), dma((7,)), dma((3,)), dma((3,)), dma((4,)), dma((4,)),
            dma((5,)), dma((5,)), dma((5,)), dma((5,)),
            dma((CHUNKS + 2,)), dma((CHUNKS + 2,)), dma((CHUNKS + 2,)), dma((CHUNKS + 2,)),
            dma((2 * TILES,)), dma((2 * TILES,)), dma((TILES + 2,)), dma((TILES + 2,)),
        ],
        compiler_params=pltpu.CompilerParams(
            collective_id=0, has_side_effects=True, vmem_limit_bytes=57 * 1024 * 1024
        ),
        name="separate",
    )(observed, valid_mask, pix_factor, col_factor)
    return pl.pallas_call(
        hand_out,
        out_shape=shapes,
        in_specs=[pl.BlockSpec(memory_space=pltpu.VMEM)] * 3,
        out_specs=[any_space] * 3,
        scratch_shapes=[dma((2 * TILES + 1,))],
        compiler_params=pltpu.CompilerParams(vmem_limit_bytes=16 * 1024 * 1024),
        name="hand_out",
    )(*results)


def solution(mesh):
    in_specs = (P("pix", "col"), P("pix", "col"), P("pix", None), P("col", None))
    out_specs = (P("pix", None), P("col", None), P("pix", "col"))
    return jax.shard_map(
        per_device, mesh=mesh, in_specs=in_specs, out_specs=out_specs, check_vma=False
    )
```

```python
import jax
import jax.numpy as jnp
from jax import lax
from jax.experimental import pallas as pl
from jax.experimental.pallas import tpu as pltpu
from jax.sharding import PartitionSpec as P

BANDS = 8
WIDTH = 256
ITERS = 2
TILE = 256
TILES = 8
CHUNKS = 16
Z_MARKS = (4, 5, 8)
AHEAD = 11

TOTAL = 67108864.0
diffusion = 0.2

f32 = jnp.float32
bf16 = jnp.bfloat16
MESH = pl.DeviceIdType.MESH


def split(x):
    hi = x.astype(bf16)
    return hi, (x - hi.astype(f32)).astype(bf16)


def left(x):
    hi, low = split(x)
    return jnp.concatenate([hi, hi, low], axis=1)


def right(x):
    hi, low = split(x)
    return jnp.concatenate([hi, low, hi], axis=0)


def mm(a, b):
    return lax.dot_general(a, b, (((1,), (0,)), ((), ())), preferred_element_type=f32)


def mm_nt(a, b):
    return lax.dot_general(a, b, (((1,), (1,)), ((), ())), preferred_element_type=f32)


def fold(x):
    part = x.reshape(x.shape[0] // 8, 8, x.shape[1]).sum(axis=0)
    return part[:, :128] + part[:, 128:]


def pack(*parts):
    rows = [jnp.sum(part, axis=0, keepdims=True) for part in parts]
    rows += [jnp.zeros((1, 128), f32)] * (4 - len(rows))
    return jnp.concatenate(rows, axis=0)


def kernel(
    obs_in, mask_in, u_in, v_in,
    u_out, vio, lay,
    r, w, c, vt, vs, hp, hsib, hf, mask, spread,
    u, us, uts, gp, gr, gt, gs, n1, n2, s1, s2, lev,
    hx, mh, uh, uhs, low_rank, low_shift, lev2, hw, way, ya, yb, yc, y_sib, p_sib, p_far, fb,
    in_sem, ss1, rs1, ss2, rs2, gss, grs, sibs, sibr,
    r1s, r1r, r2s, r2r, a2s, a2r, a1s, a1r, fs, fr,
    was, war, wbs, wbr, hys, hyr, hzs, hzr, h1s, h1r, h2s, h2r,
):
    p = lax.axis_index("pix")
    lo = lax.axis_index("col")
    core, h, z, x = p % 2, (p // 2) % 2, (p // 4) % 4, p // 16

    def dev(x, z, h, core, lo):
        return {"pix": ((x * 4 + z) * 2 + h) * 2 + core, "col": lo}

    i1 = (h * 2 + core) * 2 + lo
    i2 = x * 4 + z

    def peer1(d):
        j = (i1 + d) % 8
        return dev(x, z, j // 4, (j // 2) % 2, j % 2)

    def peer2(d):
        j = (i2 + d) % 16
        return dev(j // 4, j % 4, h, core, lo)

    sibling = dev(x, z, h, 1 - core, lo)
    col_pair = dev(x, z, h, core, 1 - lo)
    y_pair = dev(x, z, 1 - h, core, lo)
    z_next = peer2(17 - 2 * h)
    q1 = x + core * (z - x)
    q2 = z + core * (x - z)
    iy = 1 + (h + core) % 2
    iz = 3 - iy

    def ring1(q):
        return dev(q + core * (x - q), z + core * (q - z), h, core, lo)

    def ring2(q, h):
        return dev(x + core * (q - x), q + core * (z - q), h, core, lo)

    def rcopy(src, dst, send, recv, to):
        return pltpu.make_async_remote_copy(
            src_ref=src, dst_ref=dst, send_sem=send, recv_sem=recv, device_id=to, device_id_type=MESH
        )

    def each(low, high, step):
        def body(i, _):
            step(i)
            return 0

        lax.fori_loop(low, high, body, 0)

    barrier = pltpu.get_barrier_semaphore()
    for d in range(1, 8):
        pl.semaphore_signal(barrier, inc=1, device_id=peer1(d), device_id_type=MESH)
    for d in range(1, 16):
        pl.semaphore_signal(barrier, inc=1, device_id=peer2(d), device_id_type=MESH)

    loads = [pltpu.make_async_copy(v_in.at[pl.ds(t * TILE, TILE)], vio.at[t], in_sem.at[t]) for t in range(TILES)]
    loads.append(pltpu.make_async_copy(u_in, u, in_sem.at[TILES]))
    loads.append(pltpu.make_async_copy(mask_in, mask, in_sem.at[TILES + 1]))
    for t in range(TILES):
        loads.append(
            pltpu.make_async_copy(obs_in.at[:, pl.ds(t * TILE, TILE)], r.at[t], in_sem.at[TILES + 2 + t])
        )
    for load in loads:
        load.start()
    for part in range(4):
        date = lax.broadcasted_iota(jnp.int32, (128, TILE), 0)
        column = lax.broadcasted_iota(jnp.int32, (128, TILE), 1) + part * TILE
        gap = column - date * BANDS
        spread[part] = jnp.where((gap >= 0) & (gap < BANDS), 1.0, 0.0).astype(bf16)

    MASK, PIX = CHUNKS, CHUNKS + 1

    def chunk(i):
        return i // 2, pl.ds(pl.multiple_of((i % 2) * 128, 128), 128)

    def y_obs(i, slot):
        t, rows = chunk(i)
        cols = pl.ds(pl.multiple_of(t * TILE, TILE), TILE)
        return rcopy(obs_in.at[rows, cols], hx.at[slot, t, rows], hys.at[i], hyr.at[i], y_pair)

    def z_obs(i):
        t, rows = chunk(i)
        return rcopy(hx.at[iy, t, rows], hx.at[iz, t, rows], hzs.at[i], hzr.at[i], z_next)

    def ahead(i):
        t, rows = chunk(i)
        cols = pl.ds(pl.multiple_of(t * TILE, TILE), TILE)
        return rcopy(obs_in.at[rows, cols], way.at[i - AHEAD], was.at[i - AHEAD], war.at[i - AHEAD], peer2(15 + 2 * h))

    def across(i, slot):
        t, rows = chunk(i)
        return rcopy(way.at[i - AHEAD], hx.at[slot, t, rows], wbs.at[i - AHEAD], wbr.at[i - AHEAD], y_pair)

    def y_send(j):
        i = jnp.where(j < 9, j, jnp.where(j < 13, j + 3, j - 4))
        y_obs(i, iz).start()

    def z_send(i):
        y_obs(i, iy).wait_recv()
        z_obs(i).start()

    def y_mask(slot):
        return rcopy(mask_in, mh.at[slot], hys.at[MASK], hyr.at[MASK], y_pair)

    def y_pix(slot):
        return rcopy(u, uh.at[slot], hys.at[PIX], hyr.at[PIX], y_pair)

    z_mask = rcopy(mh.at[iy], mh.at[iz], hzs.at[MASK], hzr.at[MASK], z_next)
    z_pix = rcopy(uh.at[iy], uh.at[iz], hzs.at[PIX], hzr.at[PIX], z_next)
    AT = 8
    inner = pl.ds(AT, WIDTH)

    def s1_layer(t):
        return rcopy(ya.at[t, inner], y_sib.at[t], h1s.at[t], h1r.at[t], sibling)

    def s1_pass(t):
        return rcopy(yb.at[t, inner], p_sib.at[t], h1s.at[TILES + t], h1r.at[TILES + t], sibling)

    def s2_obs(t):
        return rcopy(hx.at[1, t], hx.at[0, t], h2s.at[t], h2r.at[t], sibling)

    s2_mask = rcopy(mh.at[1], mh.at[0], h2s.at[TILES], h2r.at[TILES], sibling)
    s2_pix = rcopy(uh.at[1], uh.at[0], h2s.at[TILES + 1], h2r.at[TILES + 1], sibling)

    for load in loads[: TILES]:
        load.wait()

    def turn_v(t):
        vt_t = jnp.transpose(vio[t])
        vt[t] = vt_t
        vs[t] = right(vt_t)

    each(0, TILES, turn_v)
    for load in loads[TILES:]:
        load.wait()

    def set_u(value):
        u[...] = value
        us[...] = left(value)

    set_u(u[...])

    def weight(mask_ref, t):
        dates = mask_ref[:, pl.ds(pl.multiple_of((t // 4) * 128, 128), 128)].astype(f32).astype(bf16)
        return mm(dates, spread[t % 4])

    def first(t, acc):
        w_t = weight(mask, t)
        w[t] = w_t
        r_t = w_t * (r[t] - mm(us[...], vs[t]))
        r[t] = r_t
        return acc + fold(r_t * r_t)

    zero = jnp.zeros((8, 128), f32)
    square = lax.fori_loop(0, TILES, first, zero)

    def arrived(i):
        @pl.when(i < AHEAD)
        def _():
            z_obs(i).wait_recv()

        @pl.when(i >= AHEAD)
        def _():
            y_obs(i, iy).wait_recv()
            across(i, iz).wait_recv()

    def ready(t):
        each(2 * t, 2 * t + 2, arrived)
        s2_obs(t).start()

    def turn_of(i):
        return (i + 6) % TILES

    def all_reduce(k, message, between, early=lambda: None):
        s1[k, i1] = message
        for d in range(1, 8):
            rcopy(s1.at[k, i1], s1.at[k, i1], ss1.at[k], rs1.at[k], peer1(d)).start()
        whole = s1.at[k, pl.ds(0, 7)]
        done1 = rcopy(whole, whole, ss1.at[k], rs1.at[k], sibling)
        early()
        done1.wait_recv()
        total = s1[k, 0]
        for j in range(1, 8):
            total = total + s1[k, j]
        s2[k, i2] = total
        for d in range(1, 16):
            rcopy(s2.at[k, i2], s2.at[k, i2], ss2.at[k], rs2.at[k], peer2(d)).start()
        between()
        whole = s2.at[k, pl.ds(0, 15)]
        done2 = rcopy(whole, whole, ss2.at[k], rs2.at[k], ring1((q1 + 1) % 4))
        done2.wait_recv()
        total = s2[k, 0]
        for j in range(1, 16):
            total = total + s2[k, j]
        done1.wait_send()
        done2.wait_send()
        return jnp.sum(total, axis=1, keepdims=True)

    def level_from(square):
        return jnp.sqrt(jnp.maximum(square, 0.0) / TOTAL + 1e-06)

    pl.semaphore_wait(barrier, 22)

    def begin():
        each(0, 3, y_send)

    each(AHEAD, CHUNKS - 2, lambda i: ahead(i).start())
    sums = all_reduce(0, pack(square), begin)
    lev[...] = jnp.broadcast_to(level_from(sums[0:1]), (8, 128))

    def soft(scaled):
        return scaled - jnp.minimum(jnp.maximum(scaled, -1.0), 1.0)

    def weigh(k, t):
        hw[k // 2, t] = weight(mh.at[k], t).astype(bf16)

    def set_halo(k):
        uhs[k // 2] = left(uh[k])

    def cut(value, level):
        return jnp.minimum(jnp.maximum(value, -level), level)

    mine, other = 4 * core, 4 * (1 - core)

    def y_more(low, high):
        each(jnp.minimum(low, CHUNKS), jnp.minimum(high, CHUNKS), y_send)

    def iteration(it, _):
        level = lev[0:1, 0:1]
        final = it == ITERS - 1
        y0 = 3 + CHUNKS * it

        @pl.when(final)
        def _():
            y_mask(iy).wait_recv()
            z_mask.start()

        @pl.when(it == 0)
        def _():
            ahead(CHUNKS - 2).start()

        each(Z_MARKS[0] * it, 2 + (Z_MARKS[1] - 2) * it, z_send)
        copies = []
        for part in range(2):

            def grow(t, acc):
                hi, low = split(cut(r[t], level))
                v_hi = vs[t, pl.ds(part * 128, 128)]
                v_low = vs[t, pl.ds(TILE + part * 128, 128)]
                both = mm_nt(hi, jnp.concatenate([v_hi, v_low], axis=0))
                return acc + both[:, :128] + both[:, 128:] + mm_nt(low, v_hi)

            gp[part] = lax.fori_loop(0, TILES, grow, jnp.zeros((TILE, 128), f32))
            copies.append(rcopy(gp.at[part], gr.at[part], gss.at[part], grs.at[part], col_pair))
            copies[-1].start()
        each(2 + (Z_MARKS[1] - 2) * it, 3 + (Z_MARKS[2] - 3) * it, z_send)
        for copy in copies:
            copy.wait()
        g = jnp.concatenate([gp[0] + gr[0], gp[1] + gr[1]], axis=1)
        gt[...] = g
        gs[...] = left(g)

        def curve(t, acc):
            c_t = w[t] * mm(gs[...], vs[t])
            c[t] = c_t
            return acc + fold(c_t * c_t)

        bottom = lax.fori_loop(0, TILES, curve, zero)

        @pl.when(it == 0)
        def _():
            ahead(CHUNKS - 1).start()

        def cross(i):
            ahead(i).wait_recv()
            across(i, iy).start()

        def mask_out():
            @pl.when(it == 0)
            def _():
                y_mask(iz).start()

            @pl.when(final)
            def _():
                each(AHEAD + 4, CHUNKS, cross)
                y_send(12)

        sums = all_reduce(1 + 2 * it, pack(fold(g * g) * 0.5, bottom), mask_out)
        step = sums[0:1] / sums[1:2]
        set_u(u[...] + step * gt[...])
        uts[...] = left(jnp.transpose(u[...]))

        @pl.when(final)
        def _():
            y_pix(iz).start()
            cross(AHEAD + 3)

        y_more(y0, y0 + 3)

        def pull(t):
            r_t, ac = r[t], step * c[t]
            r[t] = r_t - ac
            hp[t] = mm(uts[...], right(cut(r_t, level) - ac))

        def order(i):
            return jnp.where(i == 0, 2, jnp.where(i == 1, 1, jnp.where(i == 2, 3, 0)))

        def hand(k, slot):
            return rcopy(hp.at[other + k], hsib.at[slot], sibs.at[slot], sibr.at[slot], sibling)

        def reduce1(d):
            return rcopy(hp.at[mine + (q1 + d) % 4], n1.at[d - 1], r1s.at[d - 1], r1r.at[d - 1], ring1((q1 + d) % 4))

        def pull_step(i):
            @pl.when(i < 4)
            def _():
                d = order(i)
                pull(other + (q2 + d) % 4)
                hand((q2 + d) % 4, d).start()
                pull(mine + (q1 + d) % 4)

            @pl.when(i >= 1)
            def _():
                d = order(i - 1)
                hand(0, d).wait_recv()
                tile = mine + (q1 + d) % 4
                hp[tile] = hp[tile] + hsib[d]

                @pl.when(i < 4)
                def _():
                    reduce1(d).start()

        each(0, 5, pull_step)

        def base(k):
            set_halo(k)

            each(0, TILES, lambda t: base_tile(k, t))

        def base_tile(k, t):
            low_rank[k // 2, t] = mm(uhs[k // 2], vs[t])

        @pl.when(final)
        def _():
            z_mask.wait_recv()
            s2_mask.start()
            each(0, TILES, lambda t: weigh(2, t))
            s2_mask.wait_recv()
            each(0, TILES, lambda t: weigh(0, t))

        for d in (1, 3, 2):
            reduce1(d).wait_recv()
        tile = mine + q1
        hp[tile] = hp[tile] + n1[0] + n1[1] + n1[2]

        j2 = q2 * 2 + h

        def sub(ref, j):
            return ref.at[tile, pl.ds(pl.multiple_of(32 * j, 32), 32)]

        def reduce2(e):
            j = (j2 + e) % 8
            return rcopy(sub(hp, j), n2.at[e - 1], r2s.at[e - 1], r2r.at[e - 1], ring2(j // 2, j % 2))

        for e in range(1, 8):
            reduce2(e).start()

        @pl.when(final)
        def _():
            y_pix(iy).wait_recv()
            z_pix.start()

            @pl.when(iy == 1)
            def _():
                s2_pix.start()

            @pl.when(iy == 2)
            def _():
                base(2)

        for e in range(1, 8):
            reduce2(e).wait_recv()
        piece = sub(hp, j2)[...]
        for e in range(7):
            piece = piece + n2[e]
        sub(hf, j2)[...] = piece
        norm = fold(piece * piece)

        def gather2(e, j):
            to = (j2 + e) % 8
            return rcopy(sub(hf, j), sub(hf, j), a2s.at[e - 1], a2r.at[e - 1], ring2(to // 2, to % 2))

        def gather1(d, k):
            return rcopy(hf.at[mine + k], hf.at[mine + k], a1s.at[d - 1], a1r.at[d - 1], ring1((q1 + d) % 4))

        def onward(j):
            for d in (2, 1, 3):
                piece = sub(hf, j)
                rcopy(piece, piece, a1s.at[d - 1], a1r.at[d - 1], ring1((q1 + d) % 4)).start()

        for e in (2, 6, 4, 1, 7, 3, 5):
            gather2(e, j2).start()
        onward(j2)
        y_more(y0 + 3, y0 + 7)

        @pl.when(final)
        def _():
            each(AHEAD, AHEAD + 3, cross)
            each(13, CHUNKS, y_send)

        for n, e in enumerate((2, 6, 4, 1, 7, 3, 5)):
            j = (j2 + 8 - e) % 8
            gather2(e, j).wait_recv()
            onward(j)
            if n == 3:

                @pl.when(final)
                def _():
                    z_pix.wait_recv()

                    @pl.when(iy == 2)
                    def _():
                        s2_pix.start()

                    @pl.when(iy == 1)
                    def _():
                        set_halo(2)

            if 3 <= n < 6:

                @pl.when(final & (iy == 1))
                def _():
                    each(3 * n - 9, min(3 * n - 6, TILES), lambda t: base_tile(2, t))

        def pass_on(k, i, half):
            return rcopy(hf.at[half + k], hf.at[half + k], fs.at[i], fr.at[i], sibling)

        pass_on(q1, 0, mine).start()

        def shift(t, accs):
            s_t = w[t] * mm(us[...], right(hf[t]))
            c[t] = s_t
            r_t = r[t]
            a0, a1, a2 = accs
            return a0 + fold(r_t * r_t), a1 + fold(r_t * s_t), a2 + fold(s_t * s_t)

        def arrival(i):
            return jnp.where(i == 2, 3, jnp.where(i == 3, 2, i))

        def shift_other(i, accs):
            k = (q2 + 4 - arrival(i)) % 4
            pass_on(k, i, other).wait_recv()
            return shift(other + k, accs)

        def shift_step(i, accs):
            d = arrival(i)
            k = (q1 + 4 - d) % 4
            gather1(d, k).wait_recv()
            pass_on(k, i, mine).start()
            return shift_other(i - 1, shift(mine + k, accs))

        accs = lax.fori_loop(1, 4, shift_step, shift(mine + q1, (zero, zero, zero)))
        accs = shift_other(3, accs)
        for d in (1, 2, 3):
            reduce1(d).wait_send()
            gather1(d, q1).wait_send()
        for e in range(1, 8):
            reduce2(e).wait_send()
            gather2(e, j2).wait_send()
        for i in range(4):
            hand(i, i).wait_send()
            pass_on(i, i, mine).wait_send()
        def meanwhile():
            y_more(y0 + 7, y0 + 9)

            @pl.when(final)
            def _():
                each(0, 2, halo_shift)
                each(Z_MARKS[2] + 1, AHEAD, z_send)
                ready(turn_of(0))
                ready(turn_of(1))

        def halo_shift(k):
            def step(t):
                low_shift[k, t] = mm(uhs[k], right(hf[t]))

            each(0, TILES, step)

        def early():
            @pl.when(final)
            def _():
                s2_pix.wait_recv()
                base(0)

        z_send(jnp.where(final, Z_MARKS[2], Z_MARKS[0] - 1))
        sums = all_reduce(2 + 2 * it, pack(norm, *accs), meanwhile, early)
        step = sums[0:1] / sums[3:4]
        square = sums[1:2] - 2.0 * step * sums[2:3] + step * step * sums[3:4]
        lev[...] = jnp.broadcast_to(level_from(square), (8, 128))

        inverse = 1.0 / level_from(square)

        def update(t):
            v_t = vt[t] + step * hf[t]
            vt[t] = v_t
            vs[t] = right(v_t)
            r_t = r[t] - step * c[t]
            r[t] = r_t

            @pl.when(final)
            def _():
                ya[t, inner, :] = soft(r_t * inverse)
                s1_layer(t).start()

        each(0, TILES, update)
        lev2[...] = jnp.broadcast_to(step, (8, 128))
        return 0

    lax.fori_loop(0, ITERS, iteration, 0)
    u_out[...] = u[...]

    level = lev[0:1, 0:1]
    step_col = lev2[0:1, 0:1]
    inverse = 1.0 / level
    last = 63
    side = 1 - 2 * core

    def flag(offset):
        row = p + offset
        return ((row >= 0) & (row <= last)).astype(f32)

    has1, has2 = flag(-side), flag(-2 * side)

    def g(e):
        return e / (1.0 + e * e)

    STRIP = 32
    strips = range(0, WIDTH, STRIP)

    def rim(ref):
        ref[AT - 1 : AT, :] = ref[AT : AT + 1, :]
        ref[AT + WIDTH : AT + WIDTH + 1, :] = ref[AT + WIDTH - 1 : AT + WIDTH, :]

    def along(src, dst):
        rim(src)
        for at in range(AT, AT + WIDTH, STRIP):
            dst[pl.ds(at, STRIP), :] = g(src[pl.ds(at + 1, STRIP), :] - src[pl.ds(at, STRIP), :])

    def net(row, at):
        return fb[row, pl.ds(at + AT, STRIP), :] - fb[row, pl.ds(at + AT - 1, STRIP), :]

    def pass1(t):
        s2_obs(t).wait_recv()

        def halo(k, at):
            rows = pl.ds(at, STRIP)
            r_k = hx[2 * k, t, rows, :] - low_rank[k, t, rows, :] - step_col * low_shift[k, t, rows, :]
            return hw[k, t, rows, :].astype(f32) * soft(r_k * inverse)

        for at in strips:
            yc[pl.ds(at + AT, STRIP), :] = halo(0, at)
        along(ya.at[t], fb.at[0])
        along(yc, fb.at[1])
        s1_layer(t).wait_recv()
        for at in strips:
            rows = pl.ds(at + AT, STRIP)
            own, y1 = ya[t, rows, :], yc[rows, :]
            to1 = g(has1 * (y1 - own))
            yb[t, rows, :] = own + diffusion * (g(y_sib[t, pl.ds(at, STRIP), :] - own) + to1 + net(0, at))
            p_far[t, pl.ds(at, STRIP), :] = y1 + diffusion * (g(has2 * (halo(1, at) - y1)) - to1 + net(1, at))
        s1_pass(t).start()
        vio[t] = jnp.transpose(vt[t])

    def pass2(t):
        along(yb.at[t], fb.at[2])
        s1_pass(t).wait_recv()
        for at in strips:
            rows = pl.ds(at, STRIP)
            own = yb[t, pl.ds(at + AT, STRIP), :]
            total = g(p_sib[t, rows, :] - own) + g(has1 * (p_far[t, rows, :] - own)) + net(2, at)
            lay[t, rows, :] = level * (own + diffusion * total)

    def smooth_tile(i):
        @pl.when(i < TILES)
        def _():
            @pl.when(i + 2 < TILES)
            def _():
                ready(turn_of(i + 2))

            pass1(turn_of(i))

        @pl.when(i > 1)
        def _():
            pass2(turn_of(i - 2))

    for row in range(3):
        fb[row, :AT, :] = jnp.zeros((AT, TILE), f32)
    each(0, TILES + 2, smooth_tile)
    y_mask(iz).wait_send()
    y_pix(iz).wait_send()
    for copy in (z_mask, z_pix, s2_mask, s2_pix):
        copy.wait_send()

    def drain(i):
        y_obs(i, iz).wait_send()

        @pl.when(i < AHEAD)
        def _():
            z_obs(i).wait_send()

        @pl.when(i >= AHEAD)
        def _():
            ahead(i).wait_send()
            across(i, iy).wait_send()

    each(0, CHUNKS, drain)

    def close(t):
        s1_layer(t).wait_send()
        s1_pass(t).wait_send()
        s2_obs(t).wait_send()

    each(0, TILES, close)


def hand_out(u_in, v_in, c_in, u_out, v_out, c_out, sem):
    moves = [(u_in, u_out)]
    for t in range(TILES):
        span = pl.ds(t * TILE, TILE)
        moves += [(v_in.at[t], v_out.at[span]), (c_in.at[t], c_out.at[:, span])]
    stores = [pltpu.make_async_copy(a, b, sem.at[i]) for i, (a, b) in enumerate(moves)]
    for store in stores:
        store.start()
    for store in stores:
        store.wait()


def per_device(observed, valid_mask, pix_factor, col_factor):
    any_space = pl.BlockSpec(memory_space=pl.ANY)
    full = pltpu.VMEM((TILES, TILE, TILE), f32)
    square = pltpu.VMEM((TILE, TILE), f32)
    pair = pltpu.VMEM((TILE, 3 * TILE), bf16)
    dma = pltpu.SemaphoreType.DMA
    shapes = (
        jax.ShapeDtypeStruct((256, 256), f32),
        jax.ShapeDtypeStruct((2048, 256), f32),
        jax.ShapeDtypeStruct((256, 2048), f32),
    )
    results = pl.pallas_call(
        kernel,
        out_shape=(
            pltpu.VMEM((TILE, TILE), f32),
            pltpu.VMEM((TILES, TILE, TILE), f32),
            pltpu.VMEM((TILES, TILE, TILE), f32),
        ),
        in_specs=[any_space] * 4,
        out_specs=[pl.BlockSpec(memory_space=pltpu.VMEM)] * 3,
        scratch_shapes=[
            full, full, full, full,
            pltpu.VMEM((TILES, 3 * TILE, TILE), bf16),
            full,
            pltpu.VMEM((4, TILE, TILE), f32),
            full,
            pltpu.VMEM((256, 256), jnp.int32),
            pltpu.VMEM((4, 128, TILE), bf16),
            square, pair, pair,
            pltpu.VMEM((2, TILE, 128), f32), pltpu.VMEM((2, TILE, 128), f32),
            square, pair,
            pltpu.VMEM((3, TILE, TILE), f32),
            pltpu.VMEM((7, 32, TILE), f32),
            pltpu.VMEM((5, 8, 4, 128), f32),
            pltpu.VMEM((5, 16, 4, 128), f32),
            pltpu.VMEM((8, 128), f32),
            pltpu.VMEM((3, TILES, TILE, TILE), f32),
            pltpu.VMEM((3, 256, 256), jnp.int32),
            pltpu.VMEM((3, TILE, TILE), f32),
            pltpu.VMEM((2, TILE, 3 * TILE), bf16),
            pltpu.VMEM((2, TILES, TILE, TILE), f32),
            pltpu.VMEM((2, TILES, TILE, TILE), f32),
            pltpu.VMEM((8, 128), f32),
            pltpu.VMEM((2, TILES, TILE, TILE), bf16),
            pltpu.VMEM((CHUNKS - AHEAD, 128, TILE), f32),
            pltpu.VMEM((TILES, TILE + 16, TILE), f32),
            pltpu.VMEM((TILES, TILE + 16, TILE), f32),
            pltpu.VMEM((TILE + 16, TILE), f32),
            full, full,
            full,
            pltpu.VMEM((3, TILE + 16, TILE), f32),
            dma((2 * TILES + 2,)),
            dma((5,)), dma((5,)), dma((5,)), dma((5,)),
            dma((2,)), dma((2,)), dma((4,)), dma((4,)),
            dma((3,)), dma((3,)), dma((7,)), dma((7,)),
            dma((7,)), dma((7,)), dma((3,)), dma((3,)), dma((4,)), dma((4,)),
            dma((5,)), dma((5,)), dma((5,)), dma((5,)),
            dma((CHUNKS + 2,)), dma((CHUNKS + 2,)), dma((CHUNKS + 2,)), dma((CHUNKS + 2,)),
            dma((2 * TILES,)), dma((2 * TILES,)), dma((TILES + 2,)), dma((TILES + 2,)),
        ],
        compiler_params=pltpu.CompilerParams(
            collective_id=0, has_side_effects=True, vmem_limit_bytes=57 * 1024 * 1024
        ),
        name="separate",
    )(observed, valid_mask, pix_factor, col_factor)
    return pl.pallas_call(
        hand_out,
        out_shape=shapes,
        in_specs=[pl.BlockSpec(memory_space=pltpu.VMEM)] * 3,
        out_specs=[any_space] * 3,
        scratch_shapes=[dma((2 * TILES + 1,))],
        compiler_params=pltpu.CompilerParams(vmem_limit_bytes=16 * 1024 * 1024),
        name="hand_out",
    )(*results)


def solution(mesh):
    in_specs = (P("pix", "col"), P("pix", "col"), P("pix", None), P("col", None))
    out_specs = (P("pix", None), P("col", None), P("pix", "col"))
    return jax.shard_map(
        per_device, mesh=mesh, in_specs=in_specs, out_specs=out_specs, check_vma=False
    )
```

```python
import jax
import jax.numpy as jnp
from jax import lax
from jax.experimental import pallas as pl
from jax.experimental.pallas import tpu as pltpu
from jax.sharding import PartitionSpec as P

BANDS = 8
WIDTH = 256
ITERS = 2
TILE = 256
TILES = 8
CHUNKS = 16
Z_MARKS = (4, 4, 8)
AHEAD = 11

TOTAL = 67108864.0
diffusion = 0.2

f32 = jnp.float32
bf16 = jnp.bfloat16
MESH = pl.DeviceIdType.MESH


def split(x):
    hi = x.astype(bf16)
    return hi, (x - hi.astype(f32)).astype(bf16)


def left(x):
    hi, low = split(x)
    return jnp.concatenate([hi, hi, low], axis=1)


def right(x):
    hi, low = split(x)
    return jnp.concatenate([hi, low, hi], axis=0)


def mm(a, b):
    return lax.dot_general(a, b, (((1,), (0,)), ((), ())), preferred_element_type=f32)


def mm_nt(a, b):
    return lax.dot_general(a, b, (((1,), (1,)), ((), ())), preferred_element_type=f32)


def fold(x):
    part = x.reshape(x.shape[0] // 8, 8, x.shape[1]).sum(axis=0)
    return part[:, :128] + part[:, 128:]


def pack(*parts):
    rows = [jnp.sum(part, axis=0, keepdims=True) for part in parts]
    rows += [jnp.zeros((1, 128), f32)] * (4 - len(rows))
    return jnp.concatenate(rows, axis=0)


def kernel(
    obs_in, mask_in, u_in, v_in,
    u_out, vio, lay,
    r, w, c, vt, vs, hp, hsib, hf, mask, spread,
    u, us, uts, gp, gr, gt, gs, n1, n2, s1, s2, lev,
    hx, mh, uh, uhs, low_rank, low_shift, lev2, hw, way, ya, yb, yc, y_sib, p_sib, p_far, fb,
    in_sem, ss1, rs1, ss2, rs2, gss, grs, sibs, sibr,
    r1s, r1r, r2s, r2r, a2s, a2r, a1s, a1r, fs, fr,
    was, war, wbs, wbr, hys, hyr, hzs, hzr, h1s, h1r, h2s, h2r,
):
    p = lax.axis_index("pix")
    lo = lax.axis_index("col")
    core, h, z, x = p % 2, (p // 2) % 2, (p // 4) % 4, p // 16

    def dev(x, z, h, core, lo):
        return {"pix": ((x * 4 + z) * 2 + h) * 2 + core, "col": lo}

    i1 = (h * 2 + core) * 2 + lo
    i2 = x * 4 + z

    def peer1(d):
        j = (i1 + d) % 8
        return dev(x, z, j // 4, (j // 2) % 2, j % 2)

    def peer2(d):
        j = (i2 + d) % 16
        return dev(j // 4, j % 4, h, core, lo)

    sibling = dev(x, z, h, 1 - core, lo)
    col_pair = dev(x, z, h, core, 1 - lo)
    y_pair = dev(x, z, 1 - h, core, lo)
    z_next = peer2(17 - 2 * h)
    q1 = x + core * (z - x)
    q2 = z + core * (x - z)
    iy = 1 + (h + core) % 2
    iz = 3 - iy

    def ring1(q):
        return dev(q + core * (x - q), z + core * (q - z), h, core, lo)

    def ring2(q, h):
        return dev(x + core * (q - x), q + core * (z - q), h, core, lo)

    def rcopy(src, dst, send, recv, to):
        return pltpu.make_async_remote_copy(
            src_ref=src, dst_ref=dst, send_sem=send, recv_sem=recv, device_id=to, device_id_type=MESH
        )

    def each(low, high, step):
        def body(i, _):
            step(i)
            return 0

        lax.fori_loop(low, high, body, 0)

    barrier = pltpu.get_barrier_semaphore()
    for d in range(1, 8):
        pl.semaphore_signal(barrier, inc=1, device_id=peer1(d), device_id_type=MESH)
    for d in range(1, 16):
        pl.semaphore_signal(barrier, inc=1, device_id=peer2(d), device_id_type=MESH)

    loads = [pltpu.make_async_copy(v_in.at[pl.ds(t * TILE, TILE)], vio.at[t], in_sem.at[t]) for t in range(TILES)]
    loads.append(pltpu.make_async_copy(u_in, u, in_sem.at[TILES]))
    loads.append(pltpu.make_async_copy(mask_in, mask, in_sem.at[TILES + 1]))
    for t in range(TILES):
        loads.append(
            pltpu.make_async_copy(obs_in.at[:, pl.ds(t * TILE, TILE)], r.at[t], in_sem.at[TILES + 2 + t])
        )
    for load in loads:
        load.start()
    for part in range(4):
        date = lax.broadcasted_iota(jnp.int32, (128, TILE), 0)
        column = lax.broadcasted_iota(jnp.int32, (128, TILE), 1) + part * TILE
        gap = column - date * BANDS
        spread[part] = jnp.where((gap >= 0) & (gap < BANDS), 1.0, 0.0).astype(bf16)

    MASK, PIX = CHUNKS, CHUNKS + 1

    def chunk(i):
        return i // 2, pl.ds(pl.multiple_of((i % 2) * 128, 128), 128)

    def y_obs(i, slot):
        t, rows = chunk(i)
        cols = pl.ds(pl.multiple_of(t * TILE, TILE), TILE)
        return rcopy(obs_in.at[rows, cols], hx.at[slot, t, rows], hys.at[i], hyr.at[i], y_pair)

    def z_obs(i):
        t, rows = chunk(i)
        return rcopy(hx.at[iy, t, rows], hx.at[iz, t, rows], hzs.at[i], hzr.at[i], z_next)

    def ahead(i):
        t, rows = chunk(i)
        cols = pl.ds(pl.multiple_of(t * TILE, TILE), TILE)
        return rcopy(obs_in.at[rows, cols], way.at[i - AHEAD], was.at[i - AHEAD], war.at[i - AHEAD], peer2(15 + 2 * h))

    def across(i, slot):
        t, rows = chunk(i)
        return rcopy(way.at[i - AHEAD], hx.at[slot, t, rows], wbs.at[i - AHEAD], wbr.at[i - AHEAD], y_pair)

    def y_send(j):
        i = jnp.where(j < 9, j, jnp.where(j < 13, j + 3, j - 4))
        y_obs(i, iz).start()

    def z_send(i):
        y_obs(i, iy).wait_recv()
        z_obs(i).start()

    def y_mask(slot):
        return rcopy(mask_in, mh.at[slot], hys.at[MASK], hyr.at[MASK], y_pair)

    def y_pix(slot):
        return rcopy(u, uh.at[slot], hys.at[PIX], hyr.at[PIX], y_pair)

    z_mask = rcopy(mh.at[iy], mh.at[iz], hzs.at[MASK], hzr.at[MASK], z_next)
    z_pix = rcopy(uh.at[iy], uh.at[iz], hzs.at[PIX], hzr.at[PIX], z_next)
    AT = 8
    inner = pl.ds(AT, WIDTH)

    def s1_layer(t):
        return rcopy(ya.at[t, inner], y_sib.at[t], h1s.at[t], h1r.at[t], sibling)

    def s1_pass(t):
        return rcopy(yb.at[t, inner], p_sib.at[t], h1s.at[TILES + t], h1r.at[TILES + t], sibling)

    def s2_obs(t):
        return rcopy(hx.at[1, t], hx.at[0, t], h2s.at[t], h2r.at[t], sibling)

    s2_mask = rcopy(mh.at[1], mh.at[0], h2s.at[TILES], h2r.at[TILES], sibling)
    s2_pix = rcopy(uh.at[1], uh.at[0], h2s.at[TILES + 1], h2r.at[TILES + 1], sibling)

    for load in loads[: TILES]:
        load.wait()

    def turn_v(t):
        vt_t = jnp.transpose(vio[t])
        vt[t] = vt_t
        vs[t] = right(vt_t)

    turn_v(0)
    for load in loads[TILES : TILES + 2]:
        load.wait()

    def obs_load(t):
        cols = pl.ds(pl.multiple_of(t * TILE, TILE), TILE)
        return pltpu.make_async_copy(obs_in.at[:, cols], r.at[t], in_sem.at[TILES + 2 + t])

    def set_u(value):
        u[...] = value
        us[...] = left(value)

    set_u(u[...])

    def weight(mask_ref, t):
        dates = mask_ref[:, pl.ds(pl.multiple_of((t // 4) * 128, 128), 128)].astype(f32).astype(bf16)
        return mm(dates, spread[t % 4])

    def first(t, acc):
        obs_load(t).wait()
        w_t = weight(mask, t)
        w[t] = w_t
        r_t = w_t * (r[t] - mm(us[...], vs[t]))
        r[t] = r_t
        turn_v(jnp.minimum(t + 1, TILES - 1))
        return acc + fold(r_t * r_t)

    zero = jnp.zeros((8, 128), f32)
    square = lax.fori_loop(0, TILES, first, zero)

    def arrived(i):
        @pl.when(i < AHEAD)
        def _():
            z_obs(i).wait_recv()

        @pl.when(i >= AHEAD)
        def _():
            y_obs(i, iy).wait_recv()
            across(i, iz).wait_recv()

    def ready(t):
        each(2 * t, 2 * t + 2, arrived)
        s2_obs(t).start()

    def turn_of(i):
        return (i + 6) % TILES

    def all_reduce(k, message, between, early=lambda: None):
        s1[k, i1] = message
        for d in range(1, 8):
            rcopy(s1.at[k, i1], s1.at[k, i1], ss1.at[k], rs1.at[k], peer1(d)).start()
        whole = s1.at[k, pl.ds(0, 7)]
        done1 = rcopy(whole, whole, ss1.at[k], rs1.at[k], sibling)
        early()
        done1.wait_recv()
        total = s1[k, 0]
        for j in range(1, 8):
            total = total + s1[k, j]
        s2[k, i2] = total
        for d in range(1, 16):
            rcopy(s2.at[k, i2], s2.at[k, i2], ss2.at[k], rs2.at[k], peer2(d)).start()
        between()
        whole = s2.at[k, pl.ds(0, 15)]
        done2 = rcopy(whole, whole, ss2.at[k], rs2.at[k], ring1((q1 + 1) % 4))
        done2.wait_recv()
        total = s2[k, 0]
        for j in range(1, 16):
            total = total + s2[k, j]
        done1.wait_send()
        done2.wait_send()
        return jnp.sum(total, axis=1, keepdims=True)

    def level_from(square):
        return jnp.sqrt(jnp.maximum(square, 0.0) / TOTAL + 1e-06)

    pl.semaphore_wait(barrier, 22)

    def begin():
        each(0, 3, y_send)

    each(AHEAD, CHUNKS - 2, lambda i: ahead(i).start())
    sums = all_reduce(0, pack(square), begin)
    lev[...] = jnp.broadcast_to(level_from(sums[0:1]), (8, 128))

    def soft(scaled):
        return scaled - jnp.minimum(jnp.maximum(scaled, -1.0), 1.0)

    def weigh(k, t):
        hw[k // 2, t] = weight(mh.at[k], t).astype(bf16)

    def set_halo(k):
        uhs[k // 2] = left(uh[k])

    def cut(value, level):
        return jnp.minimum(jnp.maximum(value, -level), level)

    mine, other = 4 * core, 4 * (1 - core)

    def y_more(low, high):
        each(jnp.minimum(low, CHUNKS), jnp.minimum(high, CHUNKS), y_send)

    def iteration(it, _):
        level = lev[0:1, 0:1]
        final = it == ITERS - 1
        y0 = 3 + CHUNKS * it

        @pl.when(final)
        def _():
            y_mask(iy).wait_recv()
            z_mask.start()

        @pl.when(it == 0)
        def _():
            ahead(CHUNKS - 2).start()

        each(Z_MARKS[0] * it, 2 + (Z_MARKS[1] - 2) * it, z_send)
        copies = []
        for part in range(2):

            def grow(t, acc):
                hi, low = split(cut(r[t], level))
                v_hi = vs[t, pl.ds(part * 128, 128)]
                v_low = vs[t, pl.ds(TILE + part * 128, 128)]
                both = mm_nt(hi, jnp.concatenate([v_hi, v_low], axis=0))
                return acc + both[:, :128] + both[:, 128:] + mm_nt(low, v_hi)

            gp[part] = lax.fori_loop(0, TILES, grow, jnp.zeros((TILE, 128), f32))
            copies.append(rcopy(gp.at[part], gr.at[part], gss.at[part], grs.at[part], col_pair))
            copies[-1].start()
        each(2 + (Z_MARKS[1] - 2) * it, 3 + (Z_MARKS[2] - 3) * it, z_send)
        for copy in copies:
            copy.wait()
        g = jnp.concatenate([gp[0] + gr[0], gp[1] + gr[1]], axis=1)
        gt[...] = g
        gs[...] = left(g)

        def curve(t, acc):
            c_t = w[t] * mm(gs[...], vs[t])
            c[t] = c_t
            return acc + fold(c_t * c_t)

        bottom = lax.fori_loop(0, TILES, curve, zero)

        @pl.when(it == 0)
        def _():
            ahead(CHUNKS - 1).start()

        def cross(i):
            ahead(i).wait_recv()
            across(i, iy).start()

        def mask_out():
            @pl.when(it == 0)
            def _():
                y_mask(iz).start()

            @pl.when(final)
            def _():
                each(AHEAD + 4, CHUNKS, cross)
                y_send(12)

        sums = all_reduce(1 + 2 * it, pack(fold(g * g) * 0.5, bottom), mask_out)
        step = sums[0:1] / sums[1:2]
        set_u(u[...] + step * gt[...])
        uts[...] = left(jnp.transpose(u[...]))

        @pl.when(final)
        def _():
            y_pix(iz).start()
            cross(AHEAD + 3)

        y_more(y0, y0 + 3)

        def pull(t):
            r_t, ac = r[t], step * c[t]
            r[t] = r_t - ac
            hp[t] = mm(uts[...], right(cut(r_t, level) - ac))

        def order(i):
            return jnp.where(i == 0, 2, jnp.where(i == 1, 1, jnp.where(i == 2, 3, 0)))

        def hand(k, slot):
            return rcopy(hp.at[other + k], hsib.at[slot], sibs.at[slot], sibr.at[slot], sibling)

        def reduce1(d):
            return rcopy(hp.at[mine + (q1 + d) % 4], n1.at[d - 1], r1s.at[d - 1], r1r.at[d - 1], ring1((q1 + d) % 4))

        def pull_step(i):
            @pl.when(i < 4)
            def _():
                d = order(i)
                pull(other + (q2 + d) % 4)
                hand((q2 + d) % 4, d).start()
                pull(mine + (q1 + d) % 4)

            @pl.when(i >= 1)
            def _():
                d = order(i - 1)
                hand(0, d).wait_recv()
                tile = mine + (q1 + d) % 4
                hp[tile] = hp[tile] + hsib[d]

                @pl.when(i < 4)
                def _():
                    reduce1(d).start()

        each(0, 5, pull_step)

        def base(k):
            set_halo(k)

            each(0, TILES, lambda t: base_tile(k, t))

        def base_tile(k, t):
            low_rank[k // 2, t] = mm(uhs[k // 2], vs[t])

        @pl.when(final)
        def _():
            z_mask.wait_recv()
            s2_mask.start()
            each(0, TILES, lambda t: weigh(2, t))
            s2_mask.wait_recv()
            each(0, TILES, lambda t: weigh(0, t))

        for d in (1, 3, 2):
            reduce1(d).wait_recv()
        tile = mine + q1
        hp[tile] = hp[tile] + n1[0] + n1[1] + n1[2]

        j2 = q2 * 2 + h

        def sub(ref, j):
            return ref.at[tile, pl.ds(pl.multiple_of(32 * j, 32), 32)]

        def reduce2(e):
            j = (j2 + e) % 8
            return rcopy(sub(hp, j), n2.at[e - 1], r2s.at[e - 1], r2r.at[e - 1], ring2(j // 2, j % 2))

        for e in range(1, 8):
            reduce2(e).start()

        @pl.when(final)
        def _():
            y_pix(iy).wait_recv()
            z_pix.start()

            @pl.when(iy == 1)
            def _():
                s2_pix.start()

            @pl.when(iy == 2)
            def _():
                base(2)

        for e in range(1, 8):
            reduce2(e).wait_recv()
        piece = sub(hp, j2)[...]
        for e in range(7):
            piece = piece + n2[e]
        sub(hf, j2)[...] = piece
        norm = fold(piece * piece)

        def gather2(e, j):
            to = (j2 + e) % 8
            return rcopy(sub(hf, j), sub(hf, j), a2s.at[e - 1], a2r.at[e - 1], ring2(to // 2, to % 2))

        def gather1(d, k):
            return rcopy(hf.at[mine + k], hf.at[mine + k], a1s.at[d - 1], a1r.at[d - 1], ring1((q1 + d) % 4))

        def onward(j):
            for d in (1, 3, 2):
                piece = sub(hf, j)
                rcopy(piece, piece, a1s.at[d - 1], a1r.at[d - 1], ring1((q1 + d) % 4)).start()

        for e in (2, 6, 4, 1, 7, 3, 5):
            gather2(e, j2).start()
        onward(j2)
        y_more(y0 + 3, y0 + 7)

        @pl.when(final)
        def _():
            each(AHEAD, AHEAD + 3, cross)
            each(13, CHUNKS, y_send)

        for n, e in enumerate((2, 6, 4, 1, 7, 3, 5)):
            j = (j2 + 8 - e) % 8
            gather2(e, j).wait_recv()
            onward(j)
            if n == 3:

                @pl.when(final)
                def _():
                    z_pix.wait_recv()

                    @pl.when(iy == 2)
                    def _():
                        s2_pix.start()

                    @pl.when(iy == 1)
                    def _():
                        set_halo(2)

            if 3 <= n < 6:

                @pl.when(final & (iy == 1))
                def _():
                    each(3 * n - 9, min(3 * n - 6, TILES), lambda t: base_tile(2, t))

        def pass_on(k, i, half):
            return rcopy(hf.at[half + k], hf.at[half + k], fs.at[i], fr.at[i], sibling)

        pass_on(q1, 0, mine).start()

        def shift(t, accs):
            s_t = w[t] * mm(us[...], right(hf[t]))
            c[t] = s_t
            r_t = r[t]
            a0, a1, a2 = accs
            return a0 + fold(r_t * r_t), a1 + fold(r_t * s_t), a2 + fold(s_t * s_t)

        def arrival(i):
            return jnp.where(i == 2, 3, jnp.where(i == 3, 2, i))

        def shift_other(i, accs):
            k = (q2 + 4 - arrival(i)) % 4
            pass_on(k, i, other).wait_recv()
            return shift(other + k, accs)

        def shift_step(i, accs):
            d = arrival(i)
            k = (q1 + 4 - d) % 4
            gather1(d, k).wait_recv()
            pass_on(k, i, mine).start()
            return shift_other(i - 1, shift(mine + k, accs))

        accs = lax.fori_loop(1, 4, shift_step, shift(mine + q1, (zero, zero, zero)))
        accs = shift_other(3, accs)
        def meanwhile():
            y_more(y0 + 7, y0 + 9)

            @pl.when(final)
            def _():
                each(0, 2, halo_shift)
                each(Z_MARKS[2] + 1, AHEAD, z_send)
                ready(turn_of(0))
                ready(turn_of(1))

        def halo_shift(k):
            def step(t):
                low_shift[k, t] = mm(uhs[k], right(hf[t]))

            each(0, TILES, step)

        def early():
            for d in (1, 2, 3):
                reduce1(d).wait_send()
                gather1(d, q1).wait_send()
            for e in range(1, 8):
                reduce2(e).wait_send()
                gather2(e, j2).wait_send()
            for i in range(4):
                hand(i, i).wait_send()
                pass_on(i, i, mine).wait_send()

            @pl.when(final)
            def _():
                y_mask(iz).wait_send()
                y_pix(iz).wait_send()
                each(0, CHUNKS, lambda i: y_obs(i, iz).wait_send())
                each(AHEAD, CHUNKS, lambda i: ahead(i).wait_send())
                s2_pix.wait_recv()
                base(0)

        z_send(jnp.where(final, Z_MARKS[2], Z_MARKS[0] - 1))
        sums = all_reduce(2 + 2 * it, pack(norm, *accs), meanwhile, early)
        step = sums[0:1] / sums[3:4]
        square = sums[1:2] - 2.0 * step * sums[2:3] + step * step * sums[3:4]
        lev[...] = jnp.broadcast_to(level_from(square), (8, 128))

        inverse = 1.0 / level_from(square)

        def update(t):
            v_t = vt[t] + step * hf[t]
            vt[t] = v_t
            vs[t] = right(v_t)
            r_t = r[t] - step * c[t]
            r[t] = r_t

            @pl.when(final)
            def _():
                ya[t, inner, :] = soft(r_t * inverse)
                s1_layer(t).start()

        each(0, TILES, update)
        lev2[...] = jnp.broadcast_to(step, (8, 128))
        return 0

    lax.fori_loop(0, ITERS, iteration, 0)
    u_out[...] = u[...]

    level = lev[0:1, 0:1]
    step_col = lev2[0:1, 0:1]
    inverse = 1.0 / level
    last = 63
    side = 1 - 2 * core

    def flag(offset):
        row = p + offset
        return ((row >= 0) & (row <= last)).astype(f32)

    has1, has2 = flag(-side), flag(-2 * side)

    def g(e):
        return e / (1.0 + e * e)

    STRIP = 32
    strips = range(0, WIDTH, STRIP)

    def rim(ref):
        ref[AT - 1 : AT, :] = ref[AT : AT + 1, :]
        ref[AT + WIDTH : AT + WIDTH + 1, :] = ref[AT + WIDTH - 1 : AT + WIDTH, :]

    def along(src, dst):
        rim(src)
        for at in range(AT, AT + WIDTH, STRIP):
            dst[pl.ds(at, STRIP), :] = g(src[pl.ds(at + 1, STRIP), :] - src[pl.ds(at, STRIP), :])

    def net(row, at):
        return fb[row, pl.ds(at + AT, STRIP), :] - fb[row, pl.ds(at + AT - 1, STRIP), :]

    def pass1(t):
        s2_obs(t).wait_recv()

        def halo(k, at):
            rows = pl.ds(at, STRIP)
            r_k = hx[2 * k, t, rows, :] - low_rank[k, t, rows, :] - step_col * low_shift[k, t, rows, :]
            return hw[k, t, rows, :].astype(f32) * soft(r_k * inverse)

        for at in strips:
            yc[pl.ds(at + AT, STRIP), :] = halo(0, at)
        along(ya.at[t], fb.at[0])
        along(yc, fb.at[1])
        s1_layer(t).wait_recv()
        for at in strips:
            rows = pl.ds(at + AT, STRIP)
            own, y1 = ya[t, rows, :], yc[rows, :]
            to1 = g(has1 * (y1 - own))
            yb[t, rows, :] = own + diffusion * (g(y_sib[t, pl.ds(at, STRIP), :] - own) + to1 + net(0, at))
            p_far[t, pl.ds(at, STRIP), :] = y1 + diffusion * (g(has2 * (halo(1, at) - y1)) - to1 + net(1, at))
        s1_pass(t).start()
        vio[t] = jnp.transpose(vt[t])

    def pass2(t):
        along(yb.at[t], fb.at[2])
        s1_pass(t).wait_recv()
        for at in strips:
            rows = pl.ds(at, STRIP)
            own = yb[t, pl.ds(at + AT, STRIP), :]
            total = g(p_sib[t, rows, :] - own) + g(has1 * (p_far[t, rows, :] - own)) + net(2, at)
            lay[t, rows, :] = level * (own + diffusion * total)

    def smooth_tile(i):
        @pl.when(i < TILES)
        def _():
            @pl.when(i + 2 < TILES)
            def _():
                ready(turn_of(i + 2))

            pass1(turn_of(i))

        @pl.when(i > 1)
        def _():
            pass2(turn_of(i - 2))

    for row in range(3):
        fb[row, :AT, :] = jnp.zeros((AT, TILE), f32)
    each(0, TILES + 2, smooth_tile)
    for copy in (z_mask, z_pix, s2_mask, s2_pix):
        copy.wait_send()

    def drain(i):
        z_obs(i).wait_send()

    each(0, AHEAD, drain)
    each(AHEAD, CHUNKS, lambda i: across(i, iy).wait_send())

    def close(t):
        s1_layer(t).wait_send()
        s1_pass(t).wait_send()
        s2_obs(t).wait_send()

    each(0, TILES, close)


def hand_out(u_in, v_in, c_in, u_out, v_out, c_out, sem):
    moves = [(u_in, u_out)]
    for t in range(TILES):
        span = pl.ds(t * TILE, TILE)
        moves += [(v_in.at[t], v_out.at[span]), (c_in.at[t], c_out.at[:, span])]
    stores = [pltpu.make_async_copy(a, b, sem.at[i]) for i, (a, b) in enumerate(moves)]
    for store in stores:
        store.start()
    for store in stores:
        store.wait()


def per_device(observed, valid_mask, pix_factor, col_factor):
    any_space = pl.BlockSpec(memory_space=pl.ANY)
    full = pltpu.VMEM((TILES, TILE, TILE), f32)
    square = pltpu.VMEM((TILE, TILE), f32)
    pair = pltpu.VMEM((TILE, 3 * TILE), bf16)
    dma = pltpu.SemaphoreType.DMA
    shapes = (
        jax.ShapeDtypeStruct((256, 256), f32),
        jax.ShapeDtypeStruct((2048, 256), f32),
        jax.ShapeDtypeStruct((256, 2048), f32),
    )
    results = pl.pallas_call(
        kernel,
        out_shape=(
            pltpu.VMEM((TILE, TILE), f32),
            pltpu.VMEM((TILES, TILE, TILE), f32),
            pltpu.VMEM((TILES, TILE, TILE), f32),
        ),
        in_specs=[any_space] * 4,
        out_specs=[pl.BlockSpec(memory_space=pltpu.VMEM)] * 3,
        scratch_shapes=[
            full, full, full, full,
            pltpu.VMEM((TILES, 3 * TILE, TILE), bf16),
            full,
            pltpu.VMEM((4, TILE, TILE), f32),
            full,
            pltpu.VMEM((256, 256), jnp.int32),
            pltpu.VMEM((4, 128, TILE), bf16),
            square, pair, pair,
            pltpu.VMEM((2, TILE, 128), f32), pltpu.VMEM((2, TILE, 128), f32),
            square, pair,
            pltpu.VMEM((3, TILE, TILE), f32),
            pltpu.VMEM((7, 32, TILE), f32),
            pltpu.VMEM((5, 8, 4, 128), f32),
            pltpu.VMEM((5, 16, 4, 128), f32),
            pltpu.VMEM((8, 128), f32),
            pltpu.VMEM((3, TILES, TILE, TILE), f32),
            pltpu.VMEM((3, 256, 256), jnp.int32),
            pltpu.VMEM((3, TILE, TILE), f32),
            pltpu.VMEM((2, TILE, 3 * TILE), bf16),
            pltpu.VMEM((2, TILES, TILE, TILE), f32),
            pltpu.VMEM((2, TILES, TILE, TILE), f32),
            pltpu.VMEM((8, 128), f32),
            pltpu.VMEM((2, TILES, TILE, TILE), bf16),
            pltpu.VMEM((CHUNKS - AHEAD, 128, TILE), f32),
            pltpu.VMEM((TILES, TILE + 16, TILE), f32),
            pltpu.VMEM((TILES, TILE + 16, TILE), f32),
            pltpu.VMEM((TILE + 16, TILE), f32),
            full, full,
            full,
            pltpu.VMEM((3, TILE + 16, TILE), f32),
            dma((2 * TILES + 2,)),
            dma((5,)), dma((5,)), dma((5,)), dma((5,)),
            dma((2,)), dma((2,)), dma((4,)), dma((4,)),
            dma((3,)), dma((3,)), dma((7,)), dma((7,)),
            dma((7,)), dma((7,)), dma((3,)), dma((3,)), dma((4,)), dma((4,)),
            dma((5,)), dma((5,)), dma((5,)), dma((5,)),
            dma((CHUNKS + 2,)), dma((CHUNKS + 2,)), dma((CHUNKS + 2,)), dma((CHUNKS + 2,)),
            dma((2 * TILES,)), dma((2 * TILES,)), dma((TILES + 2,)), dma((TILES + 2,)),
        ],
        compiler_params=pltpu.CompilerParams(
            collective_id=0, has_side_effects=True, vmem_limit_bytes=57 * 1024 * 1024
        ),
        name="separate",
    )(observed, valid_mask, pix_factor, col_factor)
    return pl.pallas_call(
        hand_out,
        out_shape=shapes,
        in_specs=[pl.BlockSpec(memory_space=pltpu.VMEM)] * 3,
        out_specs=[any_space] * 3,
        scratch_shapes=[dma((2 * TILES + 1,))],
        compiler_params=pltpu.CompilerParams(vmem_limit_bytes=16 * 1024 * 1024),
        name="hand_out",
    )(*results)


def solution(mesh):
    in_specs = (P("pix", "col"), P("pix", "col"), P("pix", None), P("col", None))
    out_specs = (P("pix", None), P("col", None), P("pix", "col"))
    return jax.shard_map(
        per_device, mesh=mesh, in_specs=in_specs, out_specs=out_specs, check_vma=False
    )
```

```python
import jax
import jax.numpy as jnp
from jax import lax
from jax.experimental import pallas as pl
from jax.experimental.pallas import tpu as pltpu
from jax.sharding import PartitionSpec as P

BANDS = 8
WIDTH = 256
ITERS = 2
TILE = 256
TILES = 8
CHUNKS = 16
Z_MARKS = (4, 4, 8)
AHEAD = 11

TOTAL = 67108864.0
diffusion = 0.2

f32 = jnp.float32
bf16 = jnp.bfloat16
MESH = pl.DeviceIdType.MESH


def split(x):
    hi = x.astype(bf16)
    return hi, (x - hi.astype(f32)).astype(bf16)


def left(x):
    hi, low = split(x)
    return jnp.concatenate([hi, hi, low], axis=1)


def right(x):
    hi, low = split(x)
    return jnp.concatenate([hi, low, hi], axis=0)


def mm(a, b):
    return lax.dot_general(a, b, (((1,), (0,)), ((), ())), preferred_element_type=f32)


def mm_nt(a, b):
    return lax.dot_general(a, b, (((1,), (1,)), ((), ())), preferred_element_type=f32)


def fold(x):
    part = x.reshape(x.shape[0] // 8, 8, x.shape[1]).sum(axis=0)
    return part[:, :128] + part[:, 128:]


def pack(*parts):
    rows = [jnp.sum(part, axis=0, keepdims=True) for part in parts]
    rows += [jnp.zeros((1, 128), f32)] * (4 - len(rows))
    return jnp.concatenate(rows, axis=0)


def kernel(
    obs_in, mask_in, u_in, v_in,
    u_out, vio, lay,
    r, w, c, vt, vs, hp, hsib, hf, mask, spread,
    u, us, uts, gp, gr, gt, gs, n1, n2, s1, s2, lev,
    hx, mh, uh, uhs, low_rank, low_shift, lev2, hw, way, ya, yb, yc, y_sib, p_sib, p_far, fb,
    in_sem, ss1, rs1, ss2, rs2, gss, grs, sibs, sibr,
    r1s, r1r, r2s, r2r, a2s, a2r, a1s, a1r, fs, fr,
    was, war, wbs, wbr, hys, hyr, hzs, hzr, h1s, h1r, h2s, h2r,
):
    p = lax.axis_index("pix")
    lo = lax.axis_index("col")
    core, h, z, x = p % 2, (p // 2) % 2, (p // 4) % 4, p // 16

    def dev(x, z, h, core, lo):
        return {"pix": ((x * 4 + z) * 2 + h) * 2 + core, "col": lo}

    i1 = (h * 2 + core) * 2 + lo
    i2 = x * 4 + z

    def peer1(d):
        j = (i1 + d) % 8
        return dev(x, z, j // 4, (j // 2) % 2, j % 2)

    def peer2(d):
        j = (i2 + d) % 16
        return dev(j // 4, j % 4, h, core, lo)

    sibling = dev(x, z, h, 1 - core, lo)
    col_pair = dev(x, z, h, core, 1 - lo)
    y_pair = dev(x, z, 1 - h, core, lo)
    z_next = peer2(17 - 2 * h)
    q1 = x + core * (z - x)
    q2 = z + core * (x - z)
    iy = 1 + (h + core) % 2
    iz = 3 - iy

    def ring1(q):
        return dev(q + core * (x - q), z + core * (q - z), h, core, lo)

    def ring2(q, h):
        return dev(x + core * (q - x), q + core * (z - q), h, core, lo)

    def rcopy(src, dst, send, recv, to):
        return pltpu.make_async_remote_copy(
            src_ref=src, dst_ref=dst, send_sem=send, recv_sem=recv, device_id=to, device_id_type=MESH
        )

    def each(low, high, step):
        def body(i, _):
            step(i)
            return 0

        lax.fori_loop(low, high, body, 0)

    barrier = pltpu.get_barrier_semaphore()
    for d in range(1, 8):
        pl.semaphore_signal(barrier, inc=1, device_id=peer1(d), device_id_type=MESH)
    for d in range(1, 16):
        pl.semaphore_signal(barrier, inc=1, device_id=peer2(d), device_id_type=MESH)

    loads = [pltpu.make_async_copy(v_in.at[pl.ds(t * TILE, TILE)], vio.at[t], in_sem.at[t]) for t in range(TILES)]
    loads.append(pltpu.make_async_copy(u_in, u, in_sem.at[TILES]))
    loads.append(pltpu.make_async_copy(mask_in, mask, in_sem.at[TILES + 1]))
    for t in range(TILES):
        loads.append(
            pltpu.make_async_copy(obs_in.at[:, pl.ds(t * TILE, TILE)], r.at[t], in_sem.at[TILES + 2 + t])
        )
    for load in loads:
        load.start()
    for part in range(4):
        date = lax.broadcasted_iota(jnp.int32, (128, TILE), 0)
        column = lax.broadcasted_iota(jnp.int32, (128, TILE), 1) + part * TILE
        gap = column - date * BANDS
        spread[part] = jnp.where((gap >= 0) & (gap < BANDS), 1.0, 0.0).astype(bf16)

    MASK, PIX = CHUNKS, CHUNKS + 1

    def chunk(i):
        return i // 2, pl.ds(pl.multiple_of((i % 2) * 128, 128), 128)

    def y_obs(i, slot):
        t, rows = chunk(i)
        cols = pl.ds(pl.multiple_of(t * TILE, TILE), TILE)
        return rcopy(obs_in.at[rows, cols], hx.at[slot, t, rows], hys.at[i], hyr.at[i], y_pair)

    def z_obs(i):
        t, rows = chunk(i)
        return rcopy(hx.at[iy, t, rows], hx.at[iz, t, rows], hzs.at[i], hzr.at[i], z_next)

    def ahead(i):
        t, rows = chunk(i)
        cols = pl.ds(pl.multiple_of(t * TILE, TILE), TILE)
        return rcopy(obs_in.at[rows, cols], way.at[i - AHEAD], was.at[i - AHEAD], war.at[i - AHEAD], peer2(15 + 2 * h))

    def across(i, slot):
        t, rows = chunk(i)
        return rcopy(way.at[i - AHEAD], hx.at[slot, t, rows], wbs.at[i - AHEAD], wbr.at[i - AHEAD], y_pair)

    def y_send(j):
        i = jnp.where(j < 9, j, jnp.where(j < 13, j + 3, j - 4))
        y_obs(i, iz).start()

    def z_send(i):
        y_obs(i, iy).wait_recv()
        z_obs(i).start()

    def y_mask(slot):
        return rcopy(mask_in, mh.at[slot], hys.at[MASK], hyr.at[MASK], y_pair)

    def y_pix(slot):
        return rcopy(u, uh.at[slot], hys.at[PIX], hyr.at[PIX], y_pair)

    z_mask = rcopy(mh.at[iy], mh.at[iz], hzs.at[MASK], hzr.at[MASK], z_next)
    z_pix = rcopy(uh.at[iy], uh.at[iz], hzs.at[PIX], hzr.at[PIX], z_next)
    AT = 8
    inner = pl.ds(AT, WIDTH)

    def s1_layer(t):
        return rcopy(ya.at[t, inner], y_sib.at[t], h1s.at[t], h1r.at[t], sibling)

    def s1_pass(t):
        return rcopy(yb.at[t, inner], p_sib.at[t], h1s.at[TILES + t], h1r.at[TILES + t], sibling)

    def s2_obs(t):
        return rcopy(hx.at[1, t], hx.at[0, t], h2s.at[t], h2r.at[t], sibling)

    s2_mask = rcopy(mh.at[1], mh.at[0], h2s.at[TILES], h2r.at[TILES], sibling)
    s2_pix = rcopy(uh.at[1], uh.at[0], h2s.at[TILES + 1], h2r.at[TILES + 1], sibling)

    for load in loads[: TILES]:
        load.wait()

    def turn_v(t):
        vt_t = jnp.transpose(vio[t])
        vt[t] = vt_t
        vs[t] = right(vt_t)

    turn_v(0)
    for load in loads[TILES : TILES + 2]:
        load.wait()

    def obs_load(t):
        cols = pl.ds(pl.multiple_of(t * TILE, TILE), TILE)
        return pltpu.make_async_copy(obs_in.at[:, cols], r.at[t], in_sem.at[TILES + 2 + t])

    def set_u(value):
        u[...] = value
        us[...] = left(value)

    set_u(u[...])

    def weight(mask_ref, t):
        dates = mask_ref[:, pl.ds(pl.multiple_of((t // 4) * 128, 128), 128)].astype(f32).astype(bf16)
        return mm(dates, spread[t % 4])

    def first(t, acc):
        obs_load(t).wait()
        w_t = weight(mask, t)
        w[t] = w_t
        r_t = w_t * (r[t] - mm(us[...], vs[t]))
        r[t] = r_t
        turn_v(jnp.minimum(t + 1, TILES - 1))
        return acc + fold(r_t * r_t)

    zero = jnp.zeros((8, 128), f32)
    square = lax.fori_loop(0, TILES, first, zero)

    def arrived(i):
        @pl.when(i < AHEAD)
        def _():
            z_obs(i).wait_recv()

        @pl.when(i >= AHEAD)
        def _():
            y_obs(i, iy).wait_recv()
            across(i, iz).wait_recv()

    def ready(t):
        each(2 * t, 2 * t + 2, arrived)
        s2_obs(t).start()

    def turn_of(i):
        return (i + 6) % TILES

    def all_reduce(k, message, between, early=lambda: None):
        s1[k, i1] = message
        for d in range(1, 8):
            rcopy(s1.at[k, i1], s1.at[k, i1], ss1.at[k], rs1.at[k], peer1(d)).start()
        whole = s1.at[k, pl.ds(0, 7)]
        done1 = rcopy(whole, whole, ss1.at[k], rs1.at[k], sibling)
        early()
        done1.wait_recv()
        total = s1[k, 0]
        for j in range(1, 8):
            total = total + s1[k, j]
        s2[k, i2] = total
        for d in range(1, 16):
            rcopy(s2.at[k, i2], s2.at[k, i2], ss2.at[k], rs2.at[k], peer2(d)).start()
        between()
        whole = s2.at[k, pl.ds(0, 15)]
        done2 = rcopy(whole, whole, ss2.at[k], rs2.at[k], ring1((q1 + 1) % 4))
        done2.wait_recv()
        total = s2[k, 0]
        for j in range(1, 16):
            total = total + s2[k, j]
        done1.wait_send()
        done2.wait_send()
        return jnp.sum(total, axis=1, keepdims=True)

    def level_from(square):
        return jnp.sqrt(jnp.maximum(square, 0.0) / TOTAL + 1e-06)

    pl.semaphore_wait(barrier, 22)

    def begin():
        each(0, 3, y_send)

    each(AHEAD, CHUNKS - 2, lambda i: ahead(i).start())
    sums = all_reduce(0, pack(square), begin)
    lev[...] = jnp.broadcast_to(level_from(sums[0:1]), (8, 128))

    def soft(scaled):
        return scaled - jnp.minimum(jnp.maximum(scaled, -1.0), 1.0)

    def weigh(k, t):
        hw[k // 2, t] = weight(mh.at[k], t).astype(bf16)

    def set_halo(k):
        uhs[k // 2] = left(uh[k])

    def cut(value, level):
        return jnp.minimum(jnp.maximum(value, -level), level)

    mine, other = 4 * core, 4 * (1 - core)

    def y_more(low, high):
        each(jnp.minimum(low, CHUNKS), jnp.minimum(high, CHUNKS), y_send)

    def iteration(it, _):
        level = lev[0:1, 0:1]
        final = it == ITERS - 1
        y0 = 3 + CHUNKS * it

        @pl.when(final)
        def _():
            y_mask(iy).wait_recv()
            z_mask.start()

        @pl.when(it == 0)
        def _():
            ahead(CHUNKS - 2).start()

        each(Z_MARKS[0] * it, 2 + (Z_MARKS[1] - 2) * it, z_send)
        copies = []
        for part in range(2):

            def grow(t, acc):
                hi, low = split(cut(r[t], level))
                v_hi = vs[t, pl.ds(part * 128, 128)]
                v_low = vs[t, pl.ds(TILE + part * 128, 128)]
                both = mm_nt(hi, jnp.concatenate([v_hi, v_low], axis=0))
                return acc + both[:, :128] + both[:, 128:] + mm_nt(low, v_hi)

            gp[part] = lax.fori_loop(0, TILES, grow, jnp.zeros((TILE, 128), f32))
            copies.append(rcopy(gp.at[part], gr.at[part], gss.at[part], grs.at[part], col_pair))
            copies[-1].start()
        each(2 + (Z_MARKS[1] - 2) * it, 3 + (Z_MARKS[2] - 3) * it, z_send)
        for copy in copies:
            copy.wait()
        g = jnp.concatenate([gp[0] + gr[0], gp[1] + gr[1]], axis=1)
        gt[...] = g
        gs[...] = left(g)

        def curve(t, acc):
            c_t = w[t] * mm(gs[...], vs[t])
            c[t] = c_t
            return acc + fold(c_t * c_t)

        bottom = lax.fori_loop(0, TILES, curve, zero)

        @pl.when(it == 0)
        def _():
            ahead(CHUNKS - 1).start()

        def cross(i):
            ahead(i).wait_recv()
            across(i, iy).start()

        def mask_out():
            @pl.when(it == 0)
            def _():
                y_mask(iz).start()

            @pl.when(final)
            def _():
                each(AHEAD + 4, CHUNKS, cross)
                y_send(12)

        sums = all_reduce(1 + 2 * it, pack(fold(g * g) * 0.5, bottom), mask_out)
        step = sums[0:1] / sums[1:2]
        set_u(u[...] + step * gt[...])
        uts[...] = left(jnp.transpose(u[...]))

        @pl.when(final)
        def _():
            y_pix(iz).start()
            cross(AHEAD + 3)

        y_more(y0, y0 + 3)

        def pull(t):
            r_t, ac = r[t], step * c[t]
            r[t] = r_t - ac
            hp[t] = mm(uts[...], right(cut(r_t, level) - ac))

        def order(i):
            return jnp.where(i == 0, 2, jnp.where(i == 1, 1, jnp.where(i == 2, 3, 0)))

        def hand(k, slot):
            return rcopy(hp.at[other + k], hsib.at[slot], sibs.at[slot], sibr.at[slot], sibling)

        def reduce1(d):
            return rcopy(hp.at[mine + (q1 + d) % 4], n1.at[d - 1], r1s.at[d - 1], r1r.at[d - 1], ring1((q1 + d) % 4))

        def pull_step(i):
            @pl.when(i < 4)
            def _():
                d = order(i)
                pull(other + (q2 + d) % 4)
                hand((q2 + d) % 4, d).start()
                pull(mine + (q1 + d) % 4)

            @pl.when(i >= 1)
            def _():
                d = order(i - 1)
                hand(0, d).wait_recv()
                tile = mine + (q1 + d) % 4
                hp[tile] = hp[tile] + hsib[d]

                @pl.when(i < 4)
                def _():
                    reduce1(d).start()

        each(0, 5, pull_step)

        def base(k):
            set_halo(k)

            each(0, TILES, lambda t: base_tile(k, t))

        def base_tile(k, t):
            low_rank[k // 2, t] = mm(uhs[k // 2], vs[t])

        @pl.when(final)
        def _():
            z_mask.wait_recv()
            s2_mask.start()
            each(0, TILES, lambda t: weigh(2, t))
            s2_mask.wait_recv()
            each(0, TILES, lambda t: weigh(0, t))

        for d in (1, 3, 2):
            reduce1(d).wait_recv()
        tile = mine + q1
        hp[tile] = hp[tile] + n1[0] + n1[1] + n1[2]

        j2 = q2 * 2 + h

        def sub(ref, j):
            return ref.at[tile, pl.ds(pl.multiple_of(32 * j, 32), 32)]

        def reduce2(e):
            j = (j2 + e) % 8
            return rcopy(sub(hp, j), n2.at[e - 1], r2s.at[e - 1], r2r.at[e - 1], ring2(j // 2, j % 2))

        for e in range(1, 8):
            reduce2(e).start()

        @pl.when(final)
        def _():
            y_pix(iy).wait_recv()
            z_pix.start()

            @pl.when(iy == 1)
            def _():
                s2_pix.start()

            @pl.when(iy == 2)
            def _():
                base(2)

        for e in range(1, 8):
            reduce2(e).wait_recv()
        piece = sub(hp, j2)[...]
        for e in range(7):
            piece = piece + n2[e]
        sub(hf, j2)[...] = piece
        norm = fold(piece * piece)

        def gather2(e, j):
            to = (j2 + e) % 8
            return rcopy(sub(hf, j), sub(hf, j), a2s.at[e - 1], a2r.at[e - 1], ring2(to // 2, to % 2))

        def gather1(d, k):
            return rcopy(hf.at[mine + k], hf.at[mine + k], a1s.at[d - 1], a1r.at[d - 1], ring1((q1 + d) % 4))

        def onward(j):
            for d in (1, 3, 2):
                piece = sub(hf, j)
                rcopy(piece, piece, a1s.at[d - 1], a1r.at[d - 1], ring1((q1 + d) % 4)).start()

        for e in (2, 6, 4, 1, 7, 3, 5):
            gather2(e, j2).start()
        onward(j2)
        y_more(y0 + 3, y0 + 6)

        @pl.when(final)
        def _():
            each(AHEAD, AHEAD + 3, cross)
            each(13, CHUNKS, y_send)

        for n, e in enumerate((2, 6, 4, 1, 7, 3, 5)):
            j = (j2 + 8 - e) % 8
            gather2(e, j).wait_recv()
            onward(j)
            if n == 3:

                @pl.when(final)
                def _():
                    z_pix.wait_recv()

                    @pl.when(iy == 2)
                    def _():
                        s2_pix.start()

                    @pl.when(iy == 1)
                    def _():
                        set_halo(2)

            if 3 <= n < 6:

                @pl.when(final & (iy == 1))
                def _():
                    each(3 * n - 9, min(3 * n - 6, TILES), lambda t: base_tile(2, t))

        def pass_on(k, i, half):
            return rcopy(hf.at[half + k], hf.at[half + k], fs.at[i], fr.at[i], sibling)

        pass_on(q1, 0, mine).start()

        def shift(t, accs):
            s_t = w[t] * mm(us[...], right(hf[t]))
            c[t] = s_t
            r_t = r[t]
            a0, a1, a2 = accs
            return a0 + fold(r_t * r_t), a1 + fold(r_t * s_t), a2 + fold(s_t * s_t)

        def arrival(i):
            return jnp.where(i == 2, 3, jnp.where(i == 3, 2, i))

        def shift_other(i, accs):
            k = (q2 + 4 - arrival(i)) % 4
            pass_on(k, i, other).wait_recv()
            return shift(other + k, accs)

        def shift_step(i, accs):
            d = arrival(i)
            k = (q1 + 4 - d) % 4
            gather1(d, k).wait_recv()
            pass_on(k, i, mine).start()
            return shift_other(i - 1, shift(mine + k, accs))

        accs = lax.fori_loop(1, 4, shift_step, shift(mine + q1, (zero, zero, zero)))
        accs = shift_other(3, accs)
        def meanwhile():
            y_more(y0 + 6, y0 + 9)

            @pl.when(final)
            def _():
                each(0, 2, halo_shift)
                each(Z_MARKS[2] + 1, AHEAD, z_send)
                ready(turn_of(0))
                ready(turn_of(1))

        def halo_shift(k):
            def step(t):
                low_shift[k, t] = mm(uhs[k], right(hf[t]))

            each(0, TILES, step)

        def early():
            for d in (1, 2, 3):
                reduce1(d).wait_send()
                gather1(d, q1).wait_send()
            for e in range(1, 8):
                reduce2(e).wait_send()
                gather2(e, j2).wait_send()
            for i in range(4):
                hand(i, i).wait_send()
                pass_on(i, i, mine).wait_send()

            @pl.when(final)
            def _():
                y_mask(iz).wait_send()
                y_pix(iz).wait_send()
                each(0, CHUNKS, lambda i: y_obs(i, iz).wait_send())
                each(AHEAD, CHUNKS, lambda i: ahead(i).wait_send())
                s2_pix.wait_recv()
                base(0)

        z_send(jnp.where(final, Z_MARKS[2], Z_MARKS[0] - 1))
        sums = all_reduce(2 + 2 * it, pack(norm, *accs), meanwhile, early)
        step = sums[0:1] / sums[3:4]
        square = sums[1:2] - 2.0 * step * sums[2:3] + step * step * sums[3:4]
        lev[...] = jnp.broadcast_to(level_from(square), (8, 128))

        inverse = 1.0 / level_from(square)

        def update(t):
            v_t = vt[t] + step * hf[t]
            vt[t] = v_t
            vs[t] = right(v_t)
            r_t = r[t] - step * c[t]
            r[t] = r_t

            @pl.when(final)
            def _():
                ya[t, inner, :] = soft(r_t * inverse)
                s1_layer(t).start()

        each(0, TILES, update)
        lev2[...] = jnp.broadcast_to(step, (8, 128))
        return 0

    lax.fori_loop(0, ITERS, iteration, 0)
    u_out[...] = u[...]

    level = lev[0:1, 0:1]
    step_col = lev2[0:1, 0:1]
    inverse = 1.0 / level
    last = 63
    side = 1 - 2 * core

    def flag(offset):
        row = p + offset
        return ((row >= 0) & (row <= last)).astype(f32)

    has1, has2 = flag(-side), flag(-2 * side)

    def g(e):
        return e / (1.0 + e * e)

    STRIP = 32
    strips = range(0, WIDTH, STRIP)

    def rim(ref):
        ref[AT - 1 : AT, :] = ref[AT : AT + 1, :]
        ref[AT + WIDTH : AT + WIDTH + 1, :] = ref[AT + WIDTH - 1 : AT + WIDTH, :]

    def along(src, dst):
        rim(src)
        for at in range(AT, AT + WIDTH, STRIP):
            dst[pl.ds(at, STRIP), :] = g(src[pl.ds(at + 1, STRIP), :] - src[pl.ds(at, STRIP), :])

    def net(row, at):
        return fb[row, pl.ds(at + AT, STRIP), :] - fb[row, pl.ds(at + AT - 1, STRIP), :]

    def pass1(t):
        s2_obs(t).wait_recv()

        def halo(k, at):
            rows = pl.ds(at, STRIP)
            r_k = hx[2 * k, t, rows, :] - low_rank[k, t, rows, :] - step_col * low_shift[k, t, rows, :]
            return hw[k, t, rows, :].astype(f32) * soft(r_k * inverse)

        for at in strips:
            yc[pl.ds(at + AT, STRIP), :] = halo(0, at)
        along(ya.at[t], fb.at[0])
        along(yc, fb.at[1])
        s1_layer(t).wait_recv()
        for at in strips:
            rows = pl.ds(at + AT, STRIP)
            own, y1 = ya[t, rows, :], yc[rows, :]
            to1 = g(has1 * (y1 - own))
            yb[t, rows, :] = own + diffusion * (g(y_sib[t, pl.ds(at, STRIP), :] - own) + to1 + net(0, at))
            p_far[t, pl.ds(at, STRIP), :] = y1 + diffusion * (g(has2 * (halo(1, at) - y1)) - to1 + net(1, at))
        s1_pass(t).start()
        vio[t] = jnp.transpose(vt[t])

    def pass2(t):
        along(yb.at[t], fb.at[2])
        s1_pass(t).wait_recv()
        for at in strips:
            rows = pl.ds(at, STRIP)
            own = yb[t, pl.ds(at + AT, STRIP), :]
            total = g(p_sib[t, rows, :] - own) + g(has1 * (p_far[t, rows, :] - own)) + net(2, at)
            lay[t, rows, :] = level * (own + diffusion * total)

    def smooth_tile(i):
        @pl.when(i < TILES)
        def _():
            @pl.when(i + 2 < TILES)
            def _():
                ready(turn_of(i + 2))

            pass1(turn_of(i))

        @pl.when(i > 1)
        def _():
            pass2(turn_of(i - 2))

    for row in range(3):
        fb[row, :AT, :] = jnp.zeros((AT, TILE), f32)
    each(0, TILES + 2, smooth_tile)
    for copy in (z_mask, z_pix, s2_mask, s2_pix):
        copy.wait_send()

    def drain(i):
        z_obs(i).wait_send()

    each(0, AHEAD, drain)
    each(AHEAD, CHUNKS, lambda i: across(i, iy).wait_send())

    def close(t):
        s1_layer(t).wait_send()
        s1_pass(t).wait_send()
        s2_obs(t).wait_send()

    each(0, TILES, close)


def hand_out(u_in, v_in, c_in, u_out, v_out, c_out, sem):
    moves = [(u_in, u_out)]
    for t in range(TILES):
        span = pl.ds(t * TILE, TILE)
        moves += [(v_in.at[t], v_out.at[span]), (c_in.at[t], c_out.at[:, span])]
    stores = [pltpu.make_async_copy(a, b, sem.at[i]) for i, (a, b) in enumerate(moves)]
    for store in stores:
        store.start()
    for store in stores:
        store.wait()


def per_device(observed, valid_mask, pix_factor, col_factor):
    any_space = pl.BlockSpec(memory_space=pl.ANY)
    full = pltpu.VMEM((TILES, TILE, TILE), f32)
    square = pltpu.VMEM((TILE, TILE), f32)
    pair = pltpu.VMEM((TILE, 3 * TILE), bf16)
    dma = pltpu.SemaphoreType.DMA
    shapes = (
        jax.ShapeDtypeStruct((256, 256), f32),
        jax.ShapeDtypeStruct((2048, 256), f32),
        jax.ShapeDtypeStruct((256, 2048), f32),
    )
    results = pl.pallas_call(
        kernel,
        out_shape=(
            pltpu.VMEM((TILE, TILE), f32),
            pltpu.VMEM((TILES, TILE, TILE), f32),
            pltpu.VMEM((TILES, TILE, TILE), f32),
        ),
        in_specs=[any_space] * 4,
        out_specs=[pl.BlockSpec(memory_space=pltpu.VMEM)] * 3,
        scratch_shapes=[
            full, full, full, full,
            pltpu.VMEM((TILES, 3 * TILE, TILE), bf16),
            full,
            pltpu.VMEM((4, TILE, TILE), f32),
            full,
            pltpu.VMEM((256, 256), jnp.int32),
            pltpu.VMEM((4, 128, TILE), bf16),
            square, pair, pair,
            pltpu.VMEM((2, TILE, 128), f32), pltpu.VMEM((2, TILE, 128), f32),
            square, pair,
            pltpu.VMEM((3, TILE, TILE), f32),
            pltpu.VMEM((7, 32, TILE), f32),
            pltpu.VMEM((5, 8, 4, 128), f32),
            pltpu.VMEM((5, 16, 4, 128), f32),
            pltpu.VMEM((8, 128), f32),
            pltpu.VMEM((3, TILES, TILE, TILE), f32),
            pltpu.VMEM((3, 256, 256), jnp.int32),
            pltpu.VMEM((3, TILE, TILE), f32),
            pltpu.VMEM((2, TILE, 3 * TILE), bf16),
            pltpu.VMEM((2, TILES, TILE, TILE), f32),
            pltpu.VMEM((2, TILES, TILE, TILE), f32),
            pltpu.VMEM((8, 128), f32),
            pltpu.VMEM((2, TILES, TILE, TILE), bf16),
            pltpu.VMEM((CHUNKS - AHEAD, 128, TILE), f32),
            pltpu.VMEM((TILES, TILE + 16, TILE), f32),
            pltpu.VMEM((TILES, TILE + 16, TILE), f32),
            pltpu.VMEM((TILE + 16, TILE), f32),
            full, full,
            full,
            pltpu.VMEM((3, TILE + 16, TILE), f32),
            dma((2 * TILES + 2,)),
            dma((5,)), dma((5,)), dma((5,)), dma((5,)),
            dma((2,)), dma((2,)), dma((4,)), dma((4,)),
            dma((3,)), dma((3,)), dma((7,)), dma((7,)),
            dma((7,)), dma((7,)), dma((3,)), dma((3,)), dma((4,)), dma((4,)),
            dma((5,)), dma((5,)), dma((5,)), dma((5,)),
            dma((CHUNKS + 2,)), dma((CHUNKS + 2,)), dma((CHUNKS + 2,)), dma((CHUNKS + 2,)),
            dma((2 * TILES,)), dma((2 * TILES,)), dma((TILES + 2,)), dma((TILES + 2,)),
        ],
        compiler_params=pltpu.CompilerParams(
            collective_id=0, has_side_effects=True, vmem_limit_bytes=57 * 1024 * 1024
        ),
        name="separate",
    )(observed, valid_mask, pix_factor, col_factor)
    return pl.pallas_call(
        hand_out,
        out_shape=shapes,
        in_specs=[pl.BlockSpec(memory_space=pltpu.VMEM)] * 3,
        out_specs=[any_space] * 3,
        scratch_shapes=[dma((2 * TILES + 1,))],
        compiler_params=pltpu.CompilerParams(vmem_limit_bytes=16 * 1024 * 1024),
        name="hand_out",
    )(*results)


def solution(mesh):
    in_specs = (P("pix", "col"), P("pix", "col"), P("pix", None), P("col", None))
    out_specs = (P("pix", None), P("col", None), P("pix", "col"))
    return jax.shard_map(
        per_device, mesh=mesh, in_specs=in_specs, out_specs=out_specs, check_vma=False
    )
```
